256 devices in a mesh: gx: 4 (over z_hi), gy: 8 (over x, core), gz: 8 (over y, z_lo).
Axes of the slice: x: 4, y: 4, z: 8 (z_hi: 4, z_lo: 2; z = z_hi * 2 + z_lo), core: 2. Of those that a mesh axis runs over, the one named last changes fastest.
Arguments:
- positions: float32 [3, 4, 8, 8, 128], P(None, 'gx', 'gy', 'gz'), may hold values from 0.4 to 16.8, as said below
- species: int32 [4, 8, 8, 128], P('gx', 'gy', 'gz'), may hold values from 0 to 5, as said below
- neighbours: int32 [4, 8, 8, 26, 128], P('gx', 'gy', 'gz'), may hold values from -1 to 3328, as said below
- emb_center: float32 [5, 64], replicated, may hold values from -6 to 6
- emb_neigh: float32 [5, 64], replicated, may hold values from -6 to 6
- w_radial: float32 [8, 64], replicated, may hold values from -2 to 2
- w_two: float32 [64, 64], replicated, may hold values from -0.75 to 0.75
- w_pair: float32 [64, 384], replicated, may hold values from -0.75 to 0.75
- w_latent: float32 [256, 64], replicated, may hold values from -0.375 to 0.375
- w_out: float32 [64], replicated, may hold values from -0.75 to 0.75
Outputs:
- energies: float32 [4, 8, 8, 128], P('gx', 'gy', 'gz')
- forces: float32 [3, 4, 8, 8, 128], P(None, 'gx', 'gy', 'gz')
The draws below stay inside these ranges and needn't reach their ends.
Inputs may be any that keep to these rules, and one draw needn't show every extreme that they name: 5 marks an empty slot; other values are species. `neighbours`: entry -1 is unused; otherwise it is code * 128 + s, naming slot s of the cell whose offset (dx, dy, dz), each in -1..1, from the atom's own cell (periodic) has code = 9 (dx + 1) + 3 (dy + 1) + dz + 1. Lists are symmetric, name each neighbour once, never the atom itself or an empty slot, and are all -1 for empty slots. `positions`: offsets lie inside the cell, whose edges are 8.6, 8.6 and 17.2; any two distinct atoms are at least 0.8 apart.
All inputs are finite; a program needn't handle non-finite values.
Results may differ from the reference program's by a relative error of at most 0.0003.
Values sent between devices are 32-bit elements; how exact they have to be, the bound alone decides.
A program may use at most 128 MiB of HBM per device.

```python
import jax
import jax.numpy as jnp
import numpy as np
from jax import lax

CH = 64
NB = 8
NSPEC = 5
NX = 4
NY = 8
NZ = 8


def lattice_table():
    shifts = [(i, j, k) for i in range(-1, 2) for j in range(-1, 2) for k in range(-1, 2) if 0 < i * i + j * j + k * k <= 3]
    table = np.zeros((len(shifts), 128), np.int32)
    for atom in range(128):
        ux, uy, uz = (atom // 32, atom // 8 % 4, atom % 8)
        for entry, (i, j, k) in enumerate(shifts):
            tx, ty, tz = (ux + i, uy + j, uz + k)
            code = (tx // 4 + 1) * 9 + (ty // 4 + 1) * 3 + (tz // 8 + 1)
            slot = (tx % 4 * 4 + ty % 4) * 8 + tz % 8
            table[entry, atom] = code * 128 + slot
    return table


def species_common(key):
    return jax.random.randint(jax.random.fold_in(key, 11), (NX, NY, NZ, 128), 0, NSPEC + 1).astype(jnp.int32)


def draw_species(key, part):
    return species_common(key)


def draw_neighbours(key, part):
    kinds = species_common(key)
    live = kinds < NSPEC
    shifts = [(dx, dy, dz) for dx in (-1, 0, 1) for dy in (-1, 0, 1) for dz in (-1, 0, 1)]
    rolled = jnp.stack([jnp.roll(live, (-dx, -dy, -dz), axis=(0, 1, 2)) for dx, dy, dz in shifts], axis=3)
    rolled = rolled.reshape(NX, NY, NZ, 27 * 128)
    table = jnp.asarray(lattice_table())
    count = table.shape[0]
    target = jnp.take(rolled, table.reshape(-1), axis=3).reshape(NX, NY, NZ, count, 128)
    usable = target & live[:, :, :, None, :]
    entries = jnp.where(usable, table[None, None, None], -1)
    scores = jax.random.randint(jax.random.fold_in(key, 23), (NX, NY, NZ, count, 128), 0, 1 << 20) * 64
    scores = scores + jnp.arange(count, dtype=jnp.int32)[:, None]
    order = jnp.argsort(scores, axis=3)
    return jnp.take_along_axis(entries, order, axis=3).astype(jnp.int32)


def draw_positions(key, part):
    atom = jnp.arange(128)
    lattice = jnp.stack([atom // 32, atom // 8 % 4, atom % 8]).astype(jnp.float32)
    noise = jax.random.uniform(jax.random.fold_in(key, 5), (3, NX, NY, NZ, 128), jnp.float32, -1.0, 1.0)
    jitter = 0.3 * noise
    return ((lattice[:, None, None, None, :] + 0.5 + jitter) * 2.15).astype(jnp.float32)


def normal_values(own_key, shape, spread, most, kind=jnp.bfloat16):
    values = spread * jax.random.normal(own_key, shape, jnp.float32)
    return jnp.clip(values, min=-most, max=most).astype(kind)


def setup_inputs(seed: int = 0) -> dict:
    arg_keys = jax.random.split(jax.random.key(seed), 11)
    return {
        "positions": draw_positions(jax.random.fold_in(arg_keys[10], 71), 0),
        "species": draw_species(jax.random.fold_in(arg_keys[10], 71), 0),
        "neighbours": draw_neighbours(jax.random.fold_in(arg_keys[10], 71), 0),
        "emb_center": normal_values(arg_keys[3], (NSPEC, CH), 1.0, 6.0, jnp.float32),
        "emb_neigh": normal_values(arg_keys[4], (NSPEC, CH), 1.0, 6.0, jnp.float32),
        "w_radial": normal_values(arg_keys[5], (NB, CH), NB ** -0.5, 2.0, jnp.float32),
        "w_two": normal_values(arg_keys[6], (CH, CH), CH ** -0.5, 0.75, jnp.float32),
        "w_pair": normal_values(arg_keys[7], (CH, 6 * CH), CH ** -0.5, 0.75, jnp.float32),
        "w_latent": normal_values(arg_keys[8], (4 * CH, CH), (4 * CH) ** -0.5, 0.375, jnp.float32),
        "w_out": normal_values(arg_keys[9], (CH,), CH ** -0.5, 0.75, jnp.float32),
    }


RADIUS = 5.0
CELL_EDGES = (8.6, 8.6, 17.2)
ENVIRON_SCALE = 0.125
LEVEL_TABLE = np.array([[1, 0, 0, 0, 0, 0, 0, 0, 0], [0, 1, 1, 1, 0, 0, 0, 0, 0], [0, 0, 0, 0, 1, 1, 1, 1, 1]], np.float32)

def contract(pattern, *operands):
    return jnp.einsum(pattern, *operands, precision=lax.Precision.HIGHEST)

def harmonics(unit):
    xpart, ypart, zpart = (unit[0], unit[1], unit[2])
    root3 = np.sqrt(3.0)
    root15 = np.sqrt(15.0)
    root5 = np.sqrt(5.0)
    return jnp.stack([jnp.ones_like(xpart), root3 * xpart, root3 * ypart, root3 * zpart, root15 * xpart * ypart, root15 * ypart * zpart, 0.5 * root5 * (3.0 * zpart * zpart - 1.0), root15 * xpart * zpart, 0.5 * root15 * (xpart * xpart - ypart * ypart)])

def edge_terms(neigh, spec_neigh, center, center_embed, index, valid, weights):
    emb_center, emb_neigh, w_radial, w_two, w_pair, w_latent, w_out = weights
    width = w_two.shape[0]
    other = jnp.take(neigh, index, axis=1)
    delta = other - center[:, None, :]
    dist = jnp.sqrt(lax.optimization_barrier(jnp.sum(delta * delta, axis=0)))
    scaled = dist / RADIUS
    envelope = jnp.where(scaled < 1.0, 1.0 - 28.0 * scaled ** 6 + 48.0 * scaled ** 7 - 21.0 * scaled ** 8, 0.0) * valid
    orders = jnp.arange(1, w_radial.shape[0] + 1, dtype=jnp.float32)
    basis = np.sqrt(2.0 / RADIUS) * jnp.sin(orders[:, None, None] * np.pi * scaled[None]) / dist[None]
    harm = harmonics(delta / dist[None])
    kinds = jnp.take(spec_neigh, index)
    onehot = (kinds[None] == jnp.arange(emb_neigh.shape[0], dtype=jnp.int32)[:, None, None]).astype(jnp.float32)
    pre = contract('nc,nka->cka', w_radial, basis) + center_embed[:, None, :] + contract('sc,ska->cka', emb_neigh, onehot)
    latent = jax.nn.silu(contract('cd,cka->dka', w_two, jax.nn.silu(pre))) * envelope[None]
    mixed = contract('cd,cka->dka', w_pair, latent)
    groups = latent.shape[1]
    slots = latent.shape[2]
    env_weights = mixed[:3 * width].reshape(3, width, groups, slots)
    tp_weights = mixed[3 * width:].reshape(3, width, groups, slots)
    return (latent, envelope, harm, env_weights, tp_weights)

def cell_energy(neigh, spec_neigh, spec_center, lists, weights):
    emb_center, emb_neigh, w_radial, w_two, w_pair, w_latent, w_out = weights
    width = w_two.shape[0]
    slots = lists.shape[1]
    center = neigh[:, 13 * slots:14 * slots]
    onehot_center = (spec_center[None] == jnp.arange(emb_center.shape[0], dtype=jnp.int32)[:, None]).astype(jnp.float32)
    center_embed = contract('sc,sa->ca', emb_center, onehot_center)
    level_table = jnp.asarray(LEVEL_TABLE)
    valid = (lists >= 0).astype(jnp.float32)
    index = jnp.maximum(lists, 0).astype(jnp.int32)
    latent, envelope, harm, env_weights, tp_weights = edge_terms(neigh, spec_neigh, center, center_embed, index, valid, weights)
    environ = contract('lm,lcka,mka->cma', level_table, env_weights, harm) * ENVIRON_SCALE
    projected = contract('lm,mka,cma->lcka', level_table, harm, environ)
    scalars = (tp_weights * projected).reshape(3 * width, latent.shape[1], slots)
    joined = jnp.concatenate([latent, scalars], axis=0)
    updated = latent + jax.nn.silu(contract('cd,cka->dka', w_latent, joined))
    return lax.optimization_barrier(jnp.sum(contract('c,cka->ka', w_out, updated) * envelope, axis=0))

def cell_forces(neigh, spec_neigh, spec_center, lists, weights):
    energies, pull = jax.vjp(lambda moved: cell_energy(moved, spec_neigh, spec_center, lists, weights), neigh)
    grads = pull(jnp.ones_like(energies))[0]
    return (energies, grads)

def reference(positions, species, neighbours, emb_center, emb_neigh, w_radial, w_two, w_pair, w_latent, w_out):
    weights = (emb_center, emb_neigh, w_radial, w_two, w_pair, w_latent, w_out)
    shifts = [(dx, dy, dz) for dx in (-1, 0, 1) for dy in (-1, 0, 1) for dz in (-1, 0, 1)]
    cells = NX * NY * NZ
    slots = positions.shape[4]
    pos_slabs = []
    spec_slabs = []
    for dx, dy, dz in shifts:
        offset = jnp.asarray([dx * CELL_EDGES[0], dy * CELL_EDGES[1], dz * CELL_EDGES[2]], jnp.float32)
        pos_slabs.append(jnp.roll(positions, (-dx, -dy, -dz), axis=(1, 2, 3)) + offset[:, None, None, None, None])
        spec_slabs.append(jnp.roll(species, (-dx, -dy, -dz), axis=(0, 1, 2)))
    neigh = jnp.moveaxis(jnp.stack(pos_slabs, axis=4).reshape(3, cells, 27 * slots), 1, 0)
    spec_neigh = jnp.stack(spec_slabs, axis=3).reshape(cells, 27 * slots)
    spec_center = species.reshape(cells, slots)
    lists = neighbours.reshape(cells, neighbours.shape[3], slots)
    energies, grads = lax.map(lambda item: cell_forces(item[0], item[1], item[2], item[3], weights), (neigh, spec_neigh, spec_center, lists))
    grads = jnp.moveaxis(grads, 0, 1).reshape(3, NX, NY, NZ, 27, slots)
    total = jnp.zeros(positions.shape, jnp.float32)
    for code, (dx, dy, dz) in enumerate(shifts):
        total = total + jnp.roll(grads[:, :, :, :, code, :], (dx, dy, dz), axis=(1, 2, 3))
    return (energies.reshape(NX, NY, NZ, slots), -total)
```

```python
import functools
import math

import jax
import jax.numpy as jnp
from jax import lax
from jax.experimental import pallas as pl
from jax.experimental.pallas import tpu as pltpu
from jax.sharding import PartitionSpec as P

MESH = pl.DeviceIdType.MESH
F32 = jnp.float32
BF16 = jnp.bfloat16
RADIUS = 5.0
EDGES = (8.6, 8.6, 17.2)
SCALE = 0.125
CH = 64
SLOTS = 128
LIST = 26
PAIRS = LIST // 2
NSPEC = 5
LEVEL = (0, 1, 1, 1, 2, 2, 2, 2, 2)
SHIFTS = tuple((x, y, z) for x in (-1, 0, 1) for y in (-1, 0, 1) for z in (-1, 0, 1))
XS, INVD, ENV, KIND, HARM = 0, 1, 2, 3, 4
G_RAD, G_ENV, G_HARM = 0, 1, 2
ROOT3, ROOT5, ROOT15 = math.sqrt(3.0), math.sqrt(5.0), math.sqrt(15.0)


def split(x):
    high = x.astype(BF16)
    low = (x - high.astype(F32)).astype(BF16)
    return high, low


def stack3(x):
    high, low = split(x)
    return jnp.concatenate([high, low, high], axis=0)


def dot(lhs, rhs):
    return jnp.dot(lhs, rhs, preferred_element_type=F32)


def silu_pair(v):
    sig = 0.5 * jnp.tanh(0.5 * v) + 0.5
    act = v * sig
    return act, sig + act * (1.0 - sig)


def lanes3(high, low):
    return jnp.concatenate([high, high, low], axis=1)


def transpose_stack(w):
    high = w.astype(BF16).astype(F32)
    return jnp.concatenate([high, high, w - high], axis=0).T.astype(BF16)


def prepare_weights(w, s):
    zero = lambda rows: jnp.zeros((rows, CH), F32)
    parts = []
    radial = w["w_radial"][...]
    rh = radial.astype(BF16).astype(F32)
    parts += [rh, rh, radial - rh]
    for name in ("emb_neigh", "emb_center"):
        emb = w[name][...]
        eh = emb.astype(BF16).astype(F32)
        parts += [jnp.concatenate([eh, zero(8 - NSPEC)], axis=0)]
        parts += [jnp.concatenate([emb - eh, zero(8 - NSPEC)], axis=0)]
    parts += [zero(8)]
    s["a1"][...] = jnp.concatenate(parts, axis=0).T.astype(BF16)
    two = w["w_two"][...]
    s["a2"][...] = transpose_stack(two)
    s["a7"][...] = transpose_stack(two.T)
    s["a8"][...] = transpose_stack(radial.T)
    pair = w["w_pair"][...]
    s["a3"][...] = transpose_stack(pair)
    ph, plo = split(pair)
    s["a6"][...] = lanes3(ph, plo)
    latent = w["w_latent"][...]
    s["a4"][...] = transpose_stack(latent)
    s["a5"][...] = transpose_stack(latent.T)
    s["wout"][...] = jnp.broadcast_to(w["w_out"][...].T, (CH, SLOTS))


def geometry(table, nbr, pos, s):
    for tile in range(4):
        rows = pl.ds(tile * 8, 8)
        index = nbr[rows, :]
        valid = index >= 0
        safe = jnp.maximum(index, 0)
        code = safe >> 7
        slot = safe & 127
        got = [jnp.zeros((8, SLOTS), F32) for _ in range(4)]
        for n, shift in enumerate(SHIFTS):
            here = code == n
            for c in range(4):
                row = jnp.broadcast_to(table[n, c : c + 1, :], (8, SLOTS))
                value = jnp.take_along_axis(row, slot, axis=1, mode="promise_in_bounds")
                if c < 3 and shift[c]:
                    value = value + shift[c] * EDGES[c]
                got[c] = jnp.where(here, value, got[c])
        delta = [jnp.where(valid, got[c] - pos[c : c + 1, :], 1.0) for c in range(3)]
        square = delta[0] * delta[0] + delta[1] * delta[1] + delta[2] * delta[2]
        dist = jnp.sqrt(square)
        inv = 1.0 / dist
        ux, uy, uz = (d * inv for d in delta)
        scaled = dist * (1.0 / RADIUS)
        inside = jnp.logical_and(valid, scaled < 1.0)
        sq = scaled * scaled
        p5 = sq * sq * scaled
        p6 = p5 * scaled
        env = 1.0 + p6 * (-28.0 + scaled * (48.0 - 21.0 * scaled))
        denv = (1.0 / RADIUS) * p5 * (-168.0 + scaled * (336.0 - 168.0 * scaled))
        env = jnp.where(inside, env, 0.0)
        denv = jnp.where(inside, denv, 0.0)
        geo = s["geo"]
        values = [jnp.minimum(scaled, 1.0), inv, env, got[3]]
        values += [ROOT3 * ux, ROOT3 * uy, ROOT3 * uz, ROOT15 * ux * uy, ROOT15 * uy * uz]
        values += [0.5 * ROOT5 * (3.0 * uz * uz - 1.0), ROOT15 * ux * uz]
        values += [0.5 * ROOT15 * (ux * ux - uy * uy)]
        for r, v in enumerate(values):
            geo[rows, r, :] = v
        for r, v in enumerate((ux, uy, uz, inv, denv)):
            s["dense"][r, rows, :] = v


def pair_row(ref, i, row):
    return jnp.concatenate([ref[2 * i + j, row : row + 1, :] for j in range(2)], axis=1)


def two_body(i, s, center_hot):
    order = lax.broadcasted_iota(jnp.int32, (8, SLOTS), 0).astype(F32)
    geo = s["geo"]
    columns = []
    for j in range(2):
        k = 2 * i + j
        turns = (order + 1.0) * geo[k, XS : XS + 1, :]
        inv = geo[k, INVD : INVD + 1, :]
        whole = jnp.floor(turns + 0.5)
        part = turns - whole
        odd = whole - 2.0 * jnp.floor(0.5 * whole)
        sign = (1.0 - 2.0 * odd) * (math.sqrt(2.0 / RADIUS) * inv)
        sine, cosine = sincospi(part)
        basis = sign * sine
        s["dbas"][k] = (sign * cosine) * ((order + 1.0) * (math.pi / RADIUS)) - basis * inv
        hot = jnp.where(geo[k, KIND : KIND + 1, :] == order, 1.0, 0.0)
        high = basis.astype(BF16).astype(F32)
        zero = jnp.zeros((8, SLOTS), F32)
        columns.append(
            jnp.concatenate(
                [high, basis - high, high, hot, hot, center_hot, center_hot, zero], axis=0
            ).astype(BF16)
        )
    pre = dot(s["a1"][...], jnp.concatenate(columns, axis=1))
    act, dact = silu_pair(pre)
    s["dh"][i] = dact
    act2, dact2 = silu_pair(dot(s["a2"][...], stack3(act)))
    env = pair_row(geo, i, ENV)
    s["s2"][i] = act2
    s["d2"][i] = dact2 * env
    high, low = split(act2 * env)
    s["x1"][i, 0:CH, :] = high
    s["x1"][i, CH : 2 * CH, :] = low
    s["mix"][i] = dot(s["a3"][...], jnp.concatenate([high, low, high], axis=0))


def sincospi(part):
    t = part * math.pi
    q = t * t
    sine = 1.0 / 6227020800.0
    for c in (-1.0 / 39916800, 1.0 / 362880, -1.0 / 5040, 1.0 / 120, -1.0 / 6):
        sine = sine * q + c
    sine = t + t * (q * sine)
    cosine = -1.0 / 87178291200.0
    for c in (1.0 / 479001600, -1.0 / 3628800, 1.0 / 40320, -1.0 / 720, 1.0 / 24, -0.5, 1.0):
        cosine = cosine * q + c
    return sine, cosine


def accumulate(source, base, geo, target):
    for half in range(2):
        chan = half * 32

        def step(i, total):
            total = list(total)
            for j in range(2):
                lanes = pl.ds(j * SLOTS, SLOTS)
                parts = [source[i, pl.ds(base + l * CH + chan, 32), lanes] for l in range(3)]
                for m in range(9):
                    part = parts[LEVEL[m]]
                    if m:
                        part = part * geo[2 * i + j, HARM + m - 1 : HARM + m, :]
                    total[m] = total[m] + part
            return tuple(total)

        start = tuple(jnp.zeros((32, SLOTS), F32) for _ in range(9))
        final = lax.fori_loop(0, PAIRS, step, start)
        for m in range(9):
            target[m, pl.ds(chan, 32), :] = SCALE * final[m]


def project(i, j, geo, field):
    out = [field[0], None, None]
    for m in range(1, 9):
        term = geo[2 * i + j, HARM + m - 1 : HARM + m, :] * field[m]
        level = LEVEL[m]
        out[level] = term if out[level] is None else out[level] + term
    return jnp.concatenate(out, axis=0)


def three_body(i, energy, s):
    geo = s["geo"]
    env = pair_row(geo, i, ENV)
    proj = jnp.concatenate([project(i, j, geo, s["vec"]) for j in range(2)], axis=1)
    tensor = s["mix"][i, 3 * CH : 6 * CH, :]
    high, low = split(tensor * proj)
    x1h = s["x1"][i, 0:CH, :]
    x1l = s["x1"][i, CH : 2 * CH, :]
    z = dot(s["a4"][...], jnp.concatenate([x1h, high, x1l, low, x1h, high], axis=0))
    act, dact = silu_pair(z)
    wout = jnp.concatenate([s["wout"][...]] * 2, axis=1)
    x2 = x1h.astype(F32) + x1l.astype(F32) + act
    eps = jnp.sum(wout * x2, axis=0, keepdims=True)
    for j in range(2):
        lanes = slice(j * SLOTS, (j + 1) * SLOTS)
        s["grad"][2 * i + j, G_ENV : G_ENV + 1, :] = eps[:, lanes]
    weighted = eps * env
    energy = energy + weighted[:, :SLOTS] + weighted[:, SLOTS:]
    gout = wout * env
    gj = dot(s["a5"][...], stack3(gout * dact))
    s["gx1"][i] = gout + gj[:CH]
    gs = gj[CH:]
    ga_high, ga_low = split(gs * proj)
    s["ga"][i, 0 : 3 * CH, :] = ga_high
    s["ga"][i, 3 * CH : 6 * CH, :] = ga_low
    s["q"][i] = gs * tensor
    return energy


def backward(i, s):
    geo = s["geo"]
    ge = jnp.concatenate([project(i, j, geo, s["gvec"]) for j in range(2)], axis=1)
    high, low = split(ge)
    ga_high = s["ga"][i, 0 : 3 * CH, :]
    ga_low = s["ga"][i, 3 * CH : 6 * CH, :]
    gx1 = s["gx1"][i] + dot(
        s["a6"][...], jnp.concatenate([high, ga_high, low, ga_low, high, ga_high], axis=0)
    )
    genv = jnp.sum(gx1 * s["s2"][i], axis=0, keepdims=True)
    gh = dot(s["a7"][...], stack3(gx1 * s["d2"][i]))
    gb = dot(s["a8"][...], stack3(gh * s["dh"][i]))
    for j in range(2):
        k = 2 * i + j
        lanes = slice(j * SLOTS, (j + 1) * SLOTS)
        grad = s["grad"]
        grad[k, G_RAD : G_RAD + 1, :] = jnp.sum(gb[:, lanes] * s["dbas"][k], axis=0, keepdims=True)
        grad[k, G_ENV : G_ENV + 1, :] = grad[k, G_ENV : G_ENV + 1, :] + genv[:, lanes]
        for m in range(1, 9):
            level = LEVEL[m]
            q = s["q"][i, level * CH : (level + 1) * CH, lanes]
            e = s["mix"][i, level * CH : (level + 1) * CH, lanes]
            both = q * s["vec"][m] + e * s["gvec"][m]
            row = G_HARM + m - 1
            grad[k, row : row + 1, :] = jnp.sum(both, axis=0, keepdims=True)


def edge_forces(nbr, s):
    total = [jnp.zeros((8, SLOTS), F32) for _ in range(3)]
    for tile in range(4):
        rows = pl.ds(tile * 8, 8)
        live = s["dense"][4, rows, :] != 0.0
        valid = nbr[rows, :] >= 0
        ux, uy, uz, inv, denv = (s["dense"][r, rows, :] for r in range(5))
        grad = s["grad"]
        y = [None] + [grad[rows, G_HARM + m - 1, :] for m in range(1, 9)]
        gx = ROOT3 * y[1] + ROOT15 * (uy * y[4] + uz * y[7] + ux * y[8])
        gy = ROOT3 * y[2] + ROOT15 * (ux * y[4] + uz * y[5] - uy * y[8])
        gz = ROOT3 * y[3] + ROOT15 * (uy * y[5] + ux * y[7]) + (3.0 * ROOT5) * (uz * y[6])
        along = ux * gx + uy * gy + uz * gz
        radial = grad[rows, G_RAD, :] + grad[rows, G_ENV, :] * denv - along * inv
        for c, (unit, g) in enumerate(((ux, gx), (uy, gy), (uz, gz))):
            value = jnp.where(valid, radial * unit + g * inv, 0.0)
            s["gr"][rows, c, :] = value
            total[c] = total[c] + value
    return [jnp.sum(t, axis=0, keepdims=True) for t in total]


def scatter(i, total, nbr, s):
    lhs, rhs = [], []
    for j in range(2):
        k = 2 * i + j
        safe = jnp.maximum(nbr[pl.ds(k, 1), :], 0)
        here = lax.broadcasted_iota(jnp.int32, (32, SLOTS), 0) == (safe >> 7)
        rows = [jnp.where(here, s["gr"][k, c : c + 1, :], 0.0) for c in range(3)]
        lhs.append(jnp.concatenate(split(jnp.concatenate(rows, axis=0)), axis=0))
        slot = lax.broadcasted_iota(jnp.int32, (SLOTS, SLOTS), 0) == (safe & 127)
        rhs.append(jnp.where(slot, 1.0, 0.0).astype(BF16))
    return total + lax.dot_general(
        jnp.concatenate(lhs, axis=1),
        jnp.concatenate(rhs, axis=1),
        (((1,), (1,)), ((), ())),
        preferred_element_type=F32,
    )


def loop(count, body, start, unroll):
    blocks = count // unroll

    def block(b, carry):
        for j in range(unroll):
            carry = body(b * unroll + j, carry)
        return carry

    carry = lax.fori_loop(0, blocks, block, start)
    for i in range(blocks * unroll, count):
        carry = body(i, carry)
    return carry


def compute(table, nbr, pos, spec, s):
    geometry(table, nbr, pos, s)
    order = lax.broadcasted_iota(jnp.int32, (8, SLOTS), 0)
    center_hot = jnp.where(spec == order, 1.0, 0.0)
    nothing = lambda f: lambda i, carry: (f(i), carry)[1]
    loop(PAIRS, nothing(lambda i: two_body(i, s, center_hot)), 0, 1)
    accumulate(s["mix"], 0, s["geo"], s["vec"])
    energy = loop(PAIRS, lambda i, e: three_body(i, e, s), jnp.zeros((1, SLOTS), F32), 1)
    accumulate(s["q"], 0, s["geo"], s["gvec"])
    loop(PAIRS, nothing(lambda i: backward(i, s)), 0, 1)
    center = edge_forces(nbr, s)
    spread = loop(
        PAIRS, lambda i, t: scatter(i, t, nbr, s), jnp.zeros((192, SLOTS), F32), 1
    )
    return energy, center, spread[:96] + spread[96:]


WEIGHTS = ("emb_center", "emb_neigh", "w_radial", "w_two", "w_pair", "w_latent", "w_out")
WIDE = 2 * SLOTS
SCRATCH = {
    "a1": ((CH, 64), BF16),
    "a2": ((CH, 192), BF16),
    "a3": ((6 * CH, 192), BF16),
    "a4": ((CH, 768), BF16),
    "a5": ((4 * CH, 192), BF16),
    "a6": ((CH, 1152), BF16),
    "a7": ((CH, 192), BF16),
    "a8": ((8, 192), BF16),
    "wout": ((CH, SLOTS), F32),
    "geo": ((32, 16, SLOTS), F32),
    "dense": ((5, 32, SLOTS), F32),
    "dbas": ((LIST, 8, SLOTS), F32),
    "dh": ((PAIRS, CH, WIDE), F32),
    "s2": ((PAIRS, CH, WIDE), F32),
    "d2": ((PAIRS, CH, WIDE), F32),
    "x1": ((PAIRS, 2 * CH, WIDE), BF16),
    "mix": ((PAIRS, 6 * CH, WIDE), F32),
    "vec": ((9, CH, SLOTS), F32),
    "gvec": ((9, CH, SLOTS), F32),
    "gx1": ((PAIRS, CH, WIDE), F32),
    "ga": ((PAIRS, 6 * CH, WIDE), BF16),
    "q": ((PAIRS, 3 * CH, WIDE), F32),
    "grad": ((32, 16, SLOTS), F32),
    "gr": ((32, 8, SLOTS), F32),
    "nbr": ((32, SLOTS), jnp.int32),
}


def neighbour(shift, sizes):
    return tuple(
        lax.rem(lax.axis_index(axis) + (d + size), size)
        for (axis, size), d in zip(sizes, shift)
    )


def kernel(sizes, *refs):
    pos_in, spec_in, nbr_in = refs[:3]
    weights = dict(zip(WEIGHTS, refs[3:10]))
    energy_out, force_out = refs[10:12]
    scratch = dict(zip(SCRATCH, refs[12 : 12 + len(SCRATCH)]))
    packed, table, outbox, inbox, send, recv, send_back, recv_back = refs[12 + len(SCRATCH) :]
    others = [n for n in range(27) if n != 13]

    barrier = pltpu.get_barrier_semaphore()
    for n in others:
        pl.semaphore_signal(
            barrier, inc=1, device_id=neighbour(SHIFTS[n], sizes), device_id_type=MESH
        )
    pos = pos_in[:, 0, 0, 0, :]
    spec = spec_in[0, 0]
    mine = jnp.concatenate([pos, spec.astype(F32)], axis=0)
    packed[...] = mine
    table[13] = mine
    scratch["nbr"][...] = jnp.full((32, SLOTS), -1, jnp.int32)
    scratch["nbr"][0:LIST, :] = nbr_in[0, 0, 0]
    pl.semaphore_wait(barrier, 26)

    copies = []
    for n in others:
        copies.append(
            pltpu.make_async_remote_copy(
                src_ref=packed,
                dst_ref=table.at[26 - n],
                send_sem=send.at[n],
                recv_sem=recv.at[26 - n],
                device_id=neighbour(SHIFTS[n], sizes),
                device_id_type=MESH,
            )
        )
    for copy in copies:
        copy.start()
    prepare_weights(weights, scratch)
    for copy in copies:
        copy.wait()

    energy, center, spread = compute(table, scratch["nbr"], pos, spec, scratch)
    energy_out[0, 0] = energy
    for c in range(3):
        outbox[:, c, :] = spread[c * 32 : (c + 1) * 32]
    back = []
    for n in others:
        back.append(
            pltpu.make_async_remote_copy(
                src_ref=outbox.at[n],
                dst_ref=inbox.at[26 - n],
                send_sem=send_back.at[n],
                recv_sem=recv_back.at[26 - n],
                device_id=neighbour(SHIFTS[n], sizes),
                device_id_type=MESH,
            )
        )
    for copy in back:
        copy.start()
    force = jnp.concatenate(center, axis=0) - outbox[13, 0:3, :]
    for copy in back:
        copy.wait()
    for n in others:
        force = force - inbox[n, 0:3, :]
    force_out[:, 0, 0, 0, :] = force


def solution(mesh):
    sizes = tuple((axis, mesh.shape[axis]) for axis in ("gx", "gy", "gz"))

    def local(positions, species, neighbours, emb_c, emb_n, w_rad, w_two, w_pair, w_lat, w_out):
        vmem = pl.BlockSpec(memory_space=pltpu.VMEM)
        dma = pltpu.SemaphoreType.DMA((27,))
        return pl.pallas_call(
            functools.partial(kernel, sizes),
            out_shape=(
                jax.ShapeDtypeStruct(species.shape, F32),
                jax.ShapeDtypeStruct(positions.shape, F32),
            ),
            in_specs=[vmem] * 10,
            out_specs=(vmem, vmem),
            scratch_shapes=[pltpu.VMEM(*spec) for spec in SCRATCH.values()]
            + [
                pltpu.VMEM((4, SLOTS), F32),
                pltpu.VMEM((27, 4, SLOTS), F32),
                pltpu.VMEM((32, 8, SLOTS), F32),
                pltpu.VMEM((27, 8, SLOTS), F32),
                dma,
                dma,
                dma,
                dma,
            ],
            compiler_params=pltpu.CompilerParams(
                collective_id=0, has_side_effects=True, vmem_limit_bytes=60 << 20
            ),
        )(
            positions, species, neighbours, emb_c, emb_n, w_rad, w_two, w_pair, w_lat,
            w_out.reshape(1, CH),
        )

    placed = (
        P(None, "gx", "gy", "gz", None),
        P("gx", "gy", "gz", None),
        P("gx", "gy", "gz", None, None),
    ) + (P(),) * 7
    return jax.shard_map(
        local,
        mesh=mesh,
        in_specs=placed,
        out_specs=(P("gx", "gy", "gz", None), P(None, "gx", "gy", "gz", None)),
        check_vma=False,
    )
```

```python
import functools
import math

import jax
import jax.numpy as jnp
from jax import lax
from jax.experimental import pallas as pl
from jax.experimental.pallas import tpu as pltpu
from jax.sharding import PartitionSpec as P

MESH = pl.DeviceIdType.MESH
F32 = jnp.float32
BF16 = jnp.bfloat16
RADIUS = 5.0
EDGES = (8.6, 8.6, 17.2)
SCALE = 0.125
CH = 64
SLOTS = 128
LIST = 26
PAIRS = LIST // 2
NSPEC = 5
LEVEL = (0, 1, 1, 1, 2, 2, 2, 2, 2)
SHIFTS = tuple((x, y, z) for x in (-1, 0, 1) for y in (-1, 0, 1) for z in (-1, 0, 1))
XS, INVD, ENV, KIND, HARM = 0, 1, 2, 3, 4
G_RAD, G_ENV, G_EPS, G_HARM = 0, 1, 2, 3
GEO, PART = 16, 11
BLOCK = 16
ROOT3, ROOT5, ROOT15 = math.sqrt(3.0), math.sqrt(5.0), math.sqrt(15.0)


def split(x):
    high = x.astype(BF16)
    low = (x - high.astype(F32)).astype(BF16)
    return high, low


def stack3(x):
    high, low = split(x)
    return jnp.concatenate([high, low, high], axis=0)


def dot(lhs, rhs):
    return jnp.dot(lhs, rhs, preferred_element_type=F32)


def silu_pair(half):
    turn = jnp.tanh(half)
    act = half + half * turn
    return act, act - act * turn + turn + 1.0


def lanes3(high, low):
    return jnp.concatenate([high, high, low], axis=1)


def transpose_stack(w):
    high = w.astype(BF16).astype(F32)
    return jnp.concatenate([high, high, w - high], axis=0).T.astype(BF16)


def prepare_weights(w, s):
    zero = lambda rows: jnp.zeros((rows, CH), F32)
    parts = []
    radial = w["w_radial"][...]
    rh = radial.astype(BF16).astype(F32)
    parts += [rh, rh, radial - rh]
    for name in ("emb_neigh", "emb_center"):
        emb = w[name][...]
        eh = emb.astype(BF16).astype(F32)
        parts += [jnp.concatenate([eh, zero(8 - NSPEC)], axis=0)]
        parts += [jnp.concatenate([emb - eh, zero(8 - NSPEC)], axis=0)]
    parts += [zero(8)]
    s["a1"][...] = (0.5 * jnp.concatenate(parts, axis=0)).T.astype(BF16)
    two = w["w_two"][...]
    s["a2"][...] = transpose_stack(0.5 * two)
    s["a7"][...] = transpose_stack(0.5 * two.T)
    s["a8"][...] = transpose_stack(0.5 * radial.T)
    pair = w["w_pair"][...]
    s["a3"][...] = transpose_stack(pair)
    s["a6"][...] = lanes3(*split(pair))
    latent = w["w_latent"][...]
    s["a4"][...] = lanes3(*split(0.5 * latent))
    s["a5"][...] = transpose_stack(0.5 * latent)
    s["wout"][...] = jnp.broadcast_to(w["w_out"][...].T, (CH, SLOTS))


def geometry(table, nbr, pos, s):
    for tile in range(4):
        rows = pl.ds(tile * 8, 8)
        index = nbr[rows, :]
        valid = index >= 0
        safe = jnp.maximum(index, 0)
        code = safe >> 7
        slot = safe & 127
        got = [jnp.zeros((8, SLOTS), F32) for _ in range(4)]
        for n, shift in enumerate(SHIFTS):
            here = code == n
            for c in range(4):
                row = jnp.broadcast_to(table[n, c : c + 1, :], (8, SLOTS))
                value = jnp.take_along_axis(row, slot, axis=1, mode="promise_in_bounds")
                if c < 3 and shift[c]:
                    value = value + shift[c] * EDGES[c]
                got[c] = jnp.where(here, value, got[c])
        delta = [jnp.where(valid, got[c] - pos[c : c + 1, :], 1.0) for c in range(3)]
        square = delta[0] * delta[0] + delta[1] * delta[1] + delta[2] * delta[2]
        dist = jnp.sqrt(square)
        inv = 1.0 / dist
        ux, uy, uz = (d * inv for d in delta)
        scaled = dist * (1.0 / RADIUS)
        inside = jnp.logical_and(valid, scaled < 1.0)
        sq = scaled * scaled
        p5 = sq * sq * scaled
        p6 = p5 * scaled
        env = 1.0 + p6 * (-28.0 + scaled * (48.0 - 21.0 * scaled))
        denv = (1.0 / RADIUS) * p5 * (-168.0 + scaled * (336.0 - 168.0 * scaled))
        env = jnp.where(inside, env, 0.0)
        denv = jnp.where(inside, denv, 0.0)
        values = [jnp.minimum(scaled, 1.0), inv, env, got[3]]
        values += [ROOT3 * ux, ROOT3 * uy, ROOT3 * uz, ROOT15 * ux * uy, ROOT15 * uy * uz]
        values += [0.5 * ROOT5 * (3.0 * uz * uz - 1.0), ROOT15 * ux * uz]
        values += [0.5 * ROOT15 * (ux * ux - uy * uy)]
        for r, v in enumerate(values):
            s["geo"][pl.ds(tile * 8 * GEO + r, 8, stride=GEO), :] = v
        for r, v in enumerate((ux, uy, uz, inv, denv, env)):
            s["dense"][r, rows, :] = v


def row(s, k, r):
    return jnp.broadcast_to(s["geo"][pl.ds(k * GEO + r, 1), :], (8, SLOTS))


def tile_sum(x):
    return jnp.sum(x.reshape(x.shape[0] // 8, 8, x.shape[1]), axis=0)


def tall(tile, count):
    return jnp.concatenate([tile] * count, axis=0)


def keep(s, k, r, tile):
    s["part"][pl.ds(pl.multiple_of((k * PART + r) * 8, 8), 8), :] = tile


def two_body(i, s, center_hot):
    order = lax.broadcasted_iota(jnp.int32, (8, SLOTS), 0).astype(F32)
    columns = []
    for j in range(2):
        k = 2 * i + j
        turns = (order + 1.0) * row(s, k, XS)
        inv = row(s, k, INVD)
        whole = jnp.floor(turns + 0.5)
        part = turns - whole
        odd = whole - 2.0 * jnp.floor(0.5 * whole)
        sign = (1.0 - 2.0 * odd) * (math.sqrt(2.0 / RADIUS) * inv)
        sine, cosine = sincospi(part)
        basis = sign * sine
        s["dbas"][k] = (sign * cosine) * ((order + 1.0) * (math.pi / RADIUS)) - basis * inv
        hot = jnp.where(row(s, k, KIND) == order, 1.0, 0.0)
        high = basis.astype(BF16).astype(F32)
        zero = jnp.zeros((8, SLOTS), F32)
        columns.append(
            jnp.concatenate(
                [high, basis - high, high, hot, hot, center_hot, center_hot, zero], axis=0
            ).astype(BF16)
        )
    act, dact = silu_pair(dot(s["a1"][...], jnp.concatenate(columns, axis=1)))
    s["dh"][i] = dact
    act2, dact2 = silu_pair(dot(s["a2"][...], stack3(act)))
    env = jnp.concatenate([tall(row(s, 2 * i + j, ENV), 8) for j in range(2)], axis=1)
    s["s2"][i] = act2
    s["d2"][i] = dact2 * env
    x1 = act2 * env
    for j in range(2):
        lanes = slice(j * SLOTS, (j + 1) * SLOTS)
        keep(s, 2 * i + j, G_EPS, tile_sum(x1[:, lanes] * s["wout"][...]))
    high, low = split(x1)
    s["x1"][i, 0:CH, :] = high
    s["x1"][i, CH : 2 * CH, :] = low
    s["mix"][i] = dot(s["a3"][...], jnp.concatenate([high, low, high], axis=0))


def sincospi(part):
    t = part * math.pi
    q = t * t
    sine = 1.0 / 6227020800.0
    for c in (-1.0 / 39916800, 1.0 / 362880, -1.0 / 5040, 1.0 / 120, -1.0 / 6):
        sine = sine * q + c
    sine = t + t * (q * sine)
    cosine = -1.0 / 87178291200.0
    for c in (1.0 / 479001600, -1.0 / 3628800, 1.0 / 40320, -1.0 / 720, 1.0 / 24, -0.5, 1.0):
        cosine = cosine * q + c
    return sine, cosine


def accumulate(source, s, target):
    for block in range(CH // BLOCK):
        chan = block * BLOCK
        total = [None] * 9
        for i in range(PAIRS):
            for j in range(2):
                lanes = slice(j * SLOTS, (j + 1) * SLOTS)
                parts = [source[i, l * CH + chan : l * CH + chan + BLOCK, lanes] for l in range(3)]
                for m in range(9):
                    part = parts[LEVEL[m]]
                    if m:
                        part = part * tall(row(s, 2 * i + j, HARM + m - 1), BLOCK // 8)
                    total[m] = part if total[m] is None else total[m] + part
        for m in range(9):
            target[m, chan : chan + BLOCK, :] = SCALE * total[m]


def project(ys, fields):
    out = [fields[0], None, None]
    for m in range(1, 9):
        term = ys[m] * fields[m]
        level = LEVEL[m]
        out[level] = term if out[level] is None else out[level] + term
    return out


def harmonics_of(s, k):
    return [None] + [row(s, k, HARM + m - 1) for m in range(1, 9)]


def join(tiles):
    return jnp.concatenate(
        [jnp.concatenate([t for level in side for t in level], axis=0) for side in tiles], axis=1
    )


def three_body(i, s):
    ys = [harmonics_of(s, 2 * i + j) for j in range(2)]
    tiles = [[[] for _ in range(3)] for _ in range(2)]
    for c in range(CH // 8):
        fields = [s["vec"][m, c * 8 : c * 8 + 8, :] for m in range(9)]
        for j in range(2):
            for level, tile in enumerate(project(ys[j], fields)):
                tiles[j][level].append(tile)
    proj = join(tiles)
    tensor = s["mix"][i, 3 * CH : 6 * CH, :]
    high, low = split(tensor * proj)
    x1h = s["x1"][i, 0:CH, :]
    x1l = s["x1"][i, CH : 2 * CH, :]
    z = dot(s["a4"][...], jnp.concatenate([x1h, high, x1l, low, x1h, high], axis=0))
    act, dact = silu_pair(z)
    wout = s["wout"][...]
    for j in range(2):
        k = 2 * i + j
        lanes = slice(j * SLOTS, (j + 1) * SLOTS)
        rows = pl.ds(pl.multiple_of((k * PART + G_EPS) * 8, 8), 8)
        s["part"][rows, :] = s["part"][rows, :] + tile_sum(act[:, lanes] * wout)
    gout = jnp.concatenate([wout * tall(row(s, 2 * i + j, ENV), 8) for j in range(2)], axis=1)
    gj = dot(s["a5"][...], stack3(gout * dact))
    s["gx1"][i] = gout + gj[:CH]
    gs = gj[CH:]
    ga_high, ga_low = split(gs * proj)
    s["ga"][i, 0 : 3 * CH, :] = ga_high
    s["ga"][i, 3 * CH : 6 * CH, :] = ga_low
    s["q"][i] = gs * tensor


def backward(i, s):
    ys = [harmonics_of(s, 2 * i + j) for j in range(2)]
    tiles = [[[] for _ in range(3)] for _ in range(2)]
    turns = [[None] * 9 for _ in range(2)]
    for c in range(CH // 8):
        gfields = [s["gvec"][m, c * 8 : c * 8 + 8, :] for m in range(9)]
        fields = [None] + [s["vec"][m, c * 8 : c * 8 + 8, :] for m in range(1, 9)]
        for j in range(2):
            lanes = slice(j * SLOTS, (j + 1) * SLOTS)
            for level, tile in enumerate(project(ys[j], gfields)):
                tiles[j][level].append(tile)
            at = [slice(level * CH + c * 8, level * CH + c * 8 + 8) for level in range(3)]
            qs = [s["q"][i, a, lanes] for a in at]
            es = [s["mix"][i, a, lanes] for a in at]
            for m in range(1, 9):
                both = qs[LEVEL[m]] * fields[m] + es[LEVEL[m]] * gfields[m]
                turns[j][m] = both if c == 0 else turns[j][m] + both
    for j in range(2):
        for m in range(1, 9):
            keep(s, 2 * i + j, G_HARM + m - 1, turns[j][m])
    high, low = split(join(tiles))
    ga_high = s["ga"][i, 0 : 3 * CH, :]
    ga_low = s["ga"][i, 3 * CH : 6 * CH, :]
    gx1 = s["gx1"][i] + dot(
        s["a6"][...], jnp.concatenate([high, ga_high, low, ga_low, high, ga_high], axis=0)
    )
    genv = tile_sum(gx1 * s["s2"][i])
    gh = dot(s["a7"][...], stack3(gx1 * s["d2"][i]))
    gb = dot(s["a8"][...], stack3(gh * s["dh"][i]))
    for j in range(2):
        k = 2 * i + j
        lanes = slice(j * SLOTS, (j + 1) * SLOTS)
        keep(s, k, G_ENV, genv[:, lanes])
        keep(s, k, G_RAD, gb[:, lanes] * s["dbas"][k])


def edge_forces(nbr, s):
    total = [jnp.zeros((8, SLOTS), F32) for _ in range(4)]
    for tile in range(4):
        rows = pl.ds(tile * 8, 8)
        valid = nbr[rows, :] >= 0
        ux, uy, uz, inv, denv, env = (s["dense"][r, rows, :] for r in range(6))

        def whole(r):
            terms = [
                s["part"][pl.ds((tile * 8 * PART + r) * 8 + lane, 8, stride=8 * PART), :]
                for lane in range(8)
            ]
            while len(terms) > 1:
                terms = [a + b for a, b in zip(terms[::2], terms[1::2])]
            return terms[0]

        y = [None] + [whole(G_HARM + m - 1) for m in range(1, 9)]
        eps = whole(G_EPS)
        gx = ROOT3 * y[1] + ROOT15 * (uy * y[4] + uz * y[7] + ux * y[8])
        gy = ROOT3 * y[2] + ROOT15 * (ux * y[4] + uz * y[5] - uy * y[8])
        gz = ROOT3 * y[3] + ROOT15 * (uy * y[5] + ux * y[7]) + (3.0 * ROOT5) * (uz * y[6])
        along = ux * gx + uy * gy + uz * gz
        radial = whole(G_RAD) + (whole(G_ENV) + eps) * denv - along * inv
        for c, (unit, g) in enumerate(((ux, gx), (uy, gy), (uz, gz))):
            value = jnp.where(valid, radial * unit + g * inv, 0.0)
            s["gr"][pl.ds(tile * 64 + c, 8, stride=8), :] = value
            total[c] = total[c] + value
        total[3] = total[3] + jnp.where(valid, eps * env, 0.0)
    return [jnp.sum(t, axis=0, keepdims=True) for t in total]


def scatter(i, total, nbr, s):
    lhs, rhs = [], []
    for j in range(2):
        k = 2 * i + j
        safe = jnp.maximum(nbr[pl.ds(k, 1), :], 0)
        here = lax.broadcasted_iota(jnp.int32, (32, SLOTS), 0) == (safe >> 7)
        rows = [
            jnp.where(here, jnp.broadcast_to(s["gr"][pl.ds(k * 8 + c, 1), :], (32, SLOTS)), 0.0)
            for c in range(3)
        ]
        lhs.append(jnp.concatenate(split(jnp.concatenate(rows, axis=0)), axis=0))
        slot = lax.broadcasted_iota(jnp.int32, (SLOTS, SLOTS), 0) == (safe & 127)
        rhs.append(jnp.where(slot, 1.0, 0.0).astype(BF16))
    return total + lax.dot_general(
        jnp.concatenate(lhs, axis=1),
        jnp.concatenate(rhs, axis=1),
        (((1,), (1,)), ((), ())),
        preferred_element_type=F32,
    )


def loop(body, unroll):
    blocks = PAIRS // unroll if unroll < PAIRS else 0

    def block(b, carry):
        for j in range(unroll):
            body(b * unroll + j)
        return carry

    if blocks:
        lax.fori_loop(0, blocks, block, 0)
    for i in range(blocks * unroll, PAIRS):
        body(i)


UNROLL = (13, 13, 13)


def compute(table, nbr, pos, spec, s):
    geometry(table, nbr, pos, s)
    order = lax.broadcasted_iota(jnp.int32, (8, SLOTS), 0)
    center_hot = jnp.where(spec == order, 1.0, 0.0)
    loop(lambda i: two_body(i, s, center_hot), UNROLL[0])
    accumulate(s["mix"], s, s["vec"])
    loop(lambda i: three_body(i, s), UNROLL[1])
    accumulate(s["q"], s, s["gvec"])
    loop(lambda i: backward(i, s), UNROLL[2])
    center = edge_forces(nbr, s)
    spread = jnp.zeros((192, SLOTS), F32)
    for i in range(PAIRS):
        spread = scatter(i, spread, nbr, s)
    return center[3], center[:3], spread[:96] + spread[96:]


WEIGHTS = ("emb_center", "emb_neigh", "w_radial", "w_two", "w_pair", "w_latent", "w_out")
WIDE = 2 * SLOTS
SCRATCH = {
    "a1": ((CH, 64), BF16),
    "a2": ((CH, 192), BF16),
    "a3": ((6 * CH, 192), BF16),
    "a4": ((CH, 768), BF16),
    "a5": ((4 * CH, 192), BF16),
    "a6": ((CH, 1152), BF16),
    "a7": ((CH, 192), BF16),
    "a8": ((8, 192), BF16),
    "wout": ((CH, SLOTS), F32),
    "geo": ((32 * GEO, SLOTS), F32),
    "dense": ((6, 32, SLOTS), F32),
    "dbas": ((LIST, 8, SLOTS), F32),
    "dh": ((PAIRS, CH, WIDE), F32),
    "s2": ((PAIRS, CH, WIDE), F32),
    "d2": ((PAIRS, CH, WIDE), F32),
    "x1": ((PAIRS, 2 * CH, WIDE), BF16),
    "mix": ((PAIRS, 6 * CH, WIDE), F32),
    "vec": ((9, CH, SLOTS), F32),
    "gvec": ((9, CH, SLOTS), F32),
    "gx1": ((PAIRS, CH, WIDE), F32),
    "ga": ((PAIRS, 6 * CH, WIDE), BF16),
    "q": ((PAIRS, 3 * CH, WIDE), F32),
    "part": ((32 * PART * 8, SLOTS), F32),
    "gr": ((32 * 8, SLOTS), F32),
    "nbr": ((32, SLOTS), jnp.int32),
}


def neighbour(shift, sizes):
    return tuple(
        lax.rem(lax.axis_index(axis) + (d + size), size)
        for (axis, size), d in zip(sizes, shift)
    )


def kernel(sizes, *refs):
    pos_in, spec_in, nbr_in = refs[:3]
    weights = dict(zip(WEIGHTS, refs[3:10]))
    energy_out, force_out = refs[10:12]
    scratch = dict(zip(SCRATCH, refs[12 : 12 + len(SCRATCH)]))
    packed, table, outbox, inbox, send, recv, send_back, recv_back, list_sem = refs[12 + len(SCRATCH) :]
    others = [n for n in range(27) if n != 13]

    barrier = pltpu.get_barrier_semaphore()
    for n in others:
        pl.semaphore_signal(
            barrier, inc=1, device_id=neighbour(SHIFTS[n], sizes), device_id_type=MESH
        )
    listing = pltpu.make_async_copy(nbr_in.at[0, 0, :, 0, :], scratch["nbr"].at[0:LIST, :], list_sem)
    scratch["nbr"][LIST:, :] = jnp.full((32 - LIST, SLOTS), -1, jnp.int32)
    listing.start()
    pos = pos_in[:, 0, 0, 0, :]
    spec = spec_in[0, 0]
    mine = jnp.concatenate([pos, spec.astype(F32)], axis=0)
    packed[...] = mine
    table[13] = mine
    prepare_weights(weights, scratch)
    listing.wait()
    pl.semaphore_wait(barrier, 26)

    copies = []
    for n in others:
        copies.append(
            pltpu.make_async_remote_copy(
                src_ref=packed,
                dst_ref=table.at[26 - n],
                send_sem=send.at[n],
                recv_sem=recv.at[26 - n],
                device_id=neighbour(SHIFTS[n], sizes),
                device_id_type=MESH,
            )
        )
    for copy in copies:
        copy.start()
    for copy in copies:
        copy.wait()

    energy, center, spread = compute(table, scratch["nbr"], pos, spec, scratch)
    energy_out[0, 0] = energy
    for c in range(3):
        outbox[:, c, :] = spread[c * 32 : (c + 1) * 32]
    back = []
    for n in others:
        back.append(
            pltpu.make_async_remote_copy(
                src_ref=outbox.at[n],
                dst_ref=inbox.at[26 - n],
                send_sem=send_back.at[n],
                recv_sem=recv_back.at[26 - n],
                device_id=neighbour(SHIFTS[n], sizes),
                device_id_type=MESH,
            )
        )
    for copy in back:
        copy.start()
    force = jnp.concatenate(center, axis=0) - outbox[13, 0:3, :]
    for copy in back:
        copy.wait()
    for n in others:
        force = force - inbox[n, 0:3, :]
    force_out[:, 0, 0, 0, :] = force


def solution(mesh):
    sizes = tuple((axis, mesh.shape[axis]) for axis in ("gx", "gy", "gz"))

    def local(positions, species, neighbours, emb_c, emb_n, w_rad, w_two, w_pair, w_lat, w_out):
        vmem = pl.BlockSpec(memory_space=pltpu.VMEM)
        dma = pltpu.SemaphoreType.DMA((27,))
        return pl.pallas_call(
            functools.partial(kernel, sizes),
            out_shape=(
                jax.ShapeDtypeStruct(species.shape, F32),
                jax.ShapeDtypeStruct(positions.shape, F32),
            ),
            in_specs=[vmem] * 2 + [pl.BlockSpec(memory_space=pl.ANY)] + [vmem] * 7,
            out_specs=(vmem, vmem),
            scratch_shapes=[pltpu.VMEM(*spec) for spec in SCRATCH.values()]
            + [
                pltpu.VMEM((4, SLOTS), F32),
                pltpu.VMEM((27, 4, SLOTS), F32),
                pltpu.VMEM((32, 8, SLOTS), F32),
                pltpu.VMEM((27, 8, SLOTS), F32),
                dma,
                dma,
                dma,
                dma,
                pltpu.SemaphoreType.DMA,
            ],
            compiler_params=pltpu.CompilerParams(
                collective_id=0, has_side_effects=True, vmem_limit_bytes=60 << 20
            ),
        )(
            positions, species, jnp.swapaxes(neighbours, 2, 3), emb_c, emb_n, w_rad, w_two, w_pair,
            w_lat.T, w_out.reshape(1, CH),
        )

    placed = (
        P(None, "gx", "gy", "gz", None),
        P("gx", "gy", "gz", None),
        P("gx", "gy", "gz", None, None),
    ) + (P(),) * 7
    return jax.shard_map(
        local,
        mesh=mesh,
        in_specs=placed,
        out_specs=(P("gx", "gy", "gz", None), P(None, "gx", "gy", "gz", None)),
        check_vma=False,
    )
```

```python
import functools
import math

import jax
import jax.numpy as jnp
from jax import lax
from jax.experimental import pallas as pl
from jax.experimental.pallas import tpu as pltpu
from jax.sharding import PartitionSpec as P

MESH = pl.DeviceIdType.MESH
F32 = jnp.float32
BF16 = jnp.bfloat16
RADIUS = 5.0
EDGES = (8.6, 8.6, 17.2)
SCALE = 0.125
CH = 64
SLOTS = 128
LIST = 26
PAIRS = LIST // 2
NSPEC = 5
LEVEL = (0, 1, 1, 1, 2, 2, 2, 2, 2)
SHIFTS = tuple((x, y, z) for x in (-1, 0, 1) for y in (-1, 0, 1) for z in (-1, 0, 1))
OTHERS = [n for n in range(27) if n != 13]
PLACE = {n: place for place, n in enumerate(OTHERS)} | {13: 26}
XS, INVD, ENV, KIND, HARM = 0, 1, 2, 3, 4
G_RAD, G_ENV, G_EPS, G_HARM = 0, 1, 2, 3
GEO, PART = 16, 11
BLOCK = 16
ROOT3, ROOT5, ROOT15 = math.sqrt(3.0), math.sqrt(5.0), math.sqrt(15.0)


def split(x):
    high = x.astype(BF16)
    low = (x - high.astype(F32)).astype(BF16)
    return high, low


def stack3(x):
    high, low = split(x)
    return jnp.concatenate([high, low, high], axis=0)


def dot(lhs, rhs):
    return jnp.dot(lhs, rhs, preferred_element_type=F32)


def silu_pair(half):
    turn = jnp.tanh(half)
    act = half + half * turn
    return act, act - act * turn + turn + 1.0


def lanes3(high, low):
    return jnp.concatenate([high, high, low], axis=1)


def transpose_stack(w):
    high = w.astype(BF16).astype(F32)
    return jnp.concatenate([high, high, w - high], axis=0).T.astype(BF16)


def prepare_weights(w, s):
    zero = lambda rows: jnp.zeros((rows, CH), F32)
    parts = []
    radial = w["w_radial"][...]
    rh = radial.astype(BF16).astype(F32)
    parts += [rh, rh, radial - rh]
    for name in ("emb_neigh", "emb_center"):
        emb = w[name][...]
        eh = emb.astype(BF16).astype(F32)
        parts += [jnp.concatenate([eh, zero(8 - NSPEC)], axis=0)]
        parts += [jnp.concatenate([emb - eh, zero(8 - NSPEC)], axis=0)]
    parts += [zero(8)]
    s["a1"][...] = (0.5 * jnp.concatenate(parts, axis=0)).T.astype(BF16)
    two = w["w_two"][...]
    s["a2"][...] = transpose_stack(0.5 * two)
    s["a7"][...] = transpose_stack(0.5 * two.T)
    s["a8"][...] = transpose_stack(0.5 * radial.T)
    pair = w["w_pair"][...]
    s["a3"][...] = transpose_stack(pair[:, 3 * CH :])
    turned = pair.T
    s["a6"][...] = transpose_stack(turned[3 * CH :])
    for level in range(3):
        s["ae"][level] = transpose_stack(SCALE * pair[:, level * CH : (level + 1) * CH])
        s["ag"][level] = transpose_stack(SCALE * turned[level * CH : (level + 1) * CH])
    latent = w["w_latent"][...]
    s["a4"][...] = lanes3(*split(0.5 * latent))
    s["a5"][...] = transpose_stack(0.5 * latent)
    s["wout"][...] = jnp.broadcast_to(w["w_out"][...].T, (CH, SLOTS))


def geometry(table, nbr, pos, s):
    for tile in range(4):
        rows = pl.ds(tile * 8, 8)
        index = nbr[rows, :]
        valid = index >= 0
        safe = jnp.maximum(index, 0)
        code = safe >> 7
        slot = safe & 127
        got = [jnp.zeros((8, SLOTS), F32) for _ in range(4)]
        for n, shift in enumerate(SHIFTS):
            here = code == n
            for c in range(4):
                source = jnp.broadcast_to(table[PLACE[n], c : c + 1, :], (8, SLOTS))
                value = jnp.take_along_axis(source, slot, axis=1, mode="promise_in_bounds")
                if c < 3 and shift[c]:
                    value = value + shift[c] * EDGES[c]
                got[c] = jnp.where(here, value, got[c])
        delta = [jnp.where(valid, got[c] - pos[c : c + 1, :], 1.0) for c in range(3)]
        square = delta[0] * delta[0] + delta[1] * delta[1] + delta[2] * delta[2]
        dist = jnp.sqrt(square)
        inv = 1.0 / dist
        ux, uy, uz = (d * inv for d in delta)
        scaled = dist * (1.0 / RADIUS)
        inside = jnp.logical_and(valid, scaled < 1.0)
        sq = scaled * scaled
        p5 = sq * sq * scaled
        p6 = p5 * scaled
        env = 1.0 + p6 * (-28.0 + scaled * (48.0 - 21.0 * scaled))
        denv = (1.0 / RADIUS) * p5 * (-168.0 + scaled * (336.0 - 168.0 * scaled))
        env = jnp.where(inside, env, 0.0)
        denv = jnp.where(inside, denv, 0.0)
        values = [jnp.minimum(scaled, 1.0), inv, env, got[3]]
        values += [ROOT3 * ux, ROOT3 * uy, ROOT3 * uz, ROOT15 * ux * uy, ROOT15 * uy * uz]
        values += [0.5 * ROOT5 * (3.0 * uz * uz - 1.0), ROOT15 * ux * uz]
        values += [0.5 * ROOT15 * (ux * ux - uy * uy)]
        for r, v in enumerate(values):
            s["geo"][pl.ds(tile * 8 * GEO + r, 8, stride=GEO), :] = v
        for r, v in enumerate((ux, uy, uz, inv, denv, env)):
            s["dense"][r, rows, :] = v


def row(s, k, r):
    return jnp.broadcast_to(s["geo"][pl.ds(k * GEO + r, 1), :], (8, SLOTS))


def tile_sum(x):
    return jnp.sum(x.reshape(x.shape[0] // 8, 8, x.shape[1]), axis=0)


def tall(tile, count):
    return jnp.concatenate([tile] * count, axis=0)


def keep(s, k, r, tile):
    s["part"][pl.ds(pl.multiple_of((k * PART + r) * 8, 8), 8), :] = tile


def two_body(i, s, center_hot):
    order = lax.broadcasted_iota(jnp.int32, (8, SLOTS), 0).astype(F32)
    columns = []
    for j in range(2):
        k = 2 * i + j
        turns = (order + 1.0) * row(s, k, XS)
        inv = row(s, k, INVD)
        whole = jnp.floor(turns + 0.5)
        part = turns - whole
        odd = whole - 2.0 * jnp.floor(0.5 * whole)
        sign = (1.0 - 2.0 * odd) * (math.sqrt(2.0 / RADIUS) * inv)
        sine, cosine = sincospi(part)
        basis = sign * sine
        s["dbas"][k] = (sign * cosine) * ((order + 1.0) * (math.pi / RADIUS)) - basis * inv
        hot = jnp.where(row(s, k, KIND) == order, 1.0, 0.0)
        high = basis.astype(BF16).astype(F32)
        zero = jnp.zeros((8, SLOTS), F32)
        columns.append(
            jnp.concatenate(
                [high, basis - high, high, hot, hot, center_hot, center_hot, zero], axis=0
            ).astype(BF16)
        )
    act, dact = silu_pair(dot(s["a1"][...], jnp.concatenate(columns, axis=1)))
    s["dh"][i] = dact
    act2, dact2 = silu_pair(dot(s["a2"][...], stack3(act)))
    env = jnp.concatenate([tall(row(s, 2 * i + j, ENV), 8) for j in range(2)], axis=1)
    s["s2"][i] = act2
    s["d2"][i] = dact2 * env
    x1 = act2 * env
    for j in range(2):
        lanes = slice(j * SLOTS, (j + 1) * SLOTS)
        keep(s, 2 * i + j, G_EPS, tile_sum(x1[:, lanes] * s["wout"][...]))
    high, low = split(x1)
    s["x1f"][i] = x1
    s["x1"][i, 0:CH, :] = high
    s["x1"][i, CH : 2 * CH, :] = low
    s["mix"][i] = dot(s["a3"][...], jnp.concatenate([high, low, high], axis=0))


def sincospi(part):
    t = part * math.pi
    q = t * t
    sine = 1.0 / 6227020800.0
    for c in (-1.0 / 39916800, 1.0 / 362880, -1.0 / 5040, 1.0 / 120, -1.0 / 6):
        sine = sine * q + c
    sine = t + t * (q * sine)
    cosine = -1.0 / 87178291200.0
    for c in (1.0 / 479001600, -1.0 / 3628800, 1.0 / 40320, -1.0 / 720, 1.0 / 24, -0.5, 1.0):
        cosine = cosine * q + c
    return sine, cosine


def accumulate(source, level_rows, s, target):
    for chan in range(0, CH, BLOCK):
        total = [None] * 9
        for i in range(PAIRS):
            for j in range(2):
                lanes = slice(j * SLOTS, (j + 1) * SLOTS)
                starts = [l * level_rows + chan for l in range(3 if level_rows else 1)]
                parts = [source[i, a : a + BLOCK, lanes] for a in starts]
                for m in range(9):
                    part = parts[LEVEL[m] if level_rows else 0]
                    if m:
                        part = part * tall(row(s, 2 * i + j, HARM + m - 1), BLOCK // 8)
                    total[m] = part if total[m] is None else total[m] + part
        for m in range(9):
            target[chan : chan + BLOCK, m * SLOTS : (m + 1) * SLOTS] = total[m]


def mix_levels(weights, source, target):
    for level, (low, high) in enumerate(((0, 1), (1, 4), (4, 9))):
        lanes = slice(low * SLOTS, high * SLOTS)
        mixed = dot(weights[level], stack3(source[:, lanes]))
        for m in range(low, high):
            target[m] = mixed[:, (m - low) * SLOTS : (m - low + 1) * SLOTS]


def project(ys, fields):
    out = [fields[0], None, None]
    for m in range(1, 9):
        term = ys[m] * fields[m]
        level = LEVEL[m]
        out[level] = term if out[level] is None else out[level] + term
    return out


def harmonics_of(s, k):
    return [None] + [row(s, k, HARM + m - 1) for m in range(1, 9)]


def join(tiles):
    return jnp.concatenate(
        [jnp.concatenate([t for level in side for t in level], axis=0) for side in tiles], axis=1
    )


def three_body(i, s):
    ys = [harmonics_of(s, 2 * i + j) for j in range(2)]
    tiles = [[[] for _ in range(3)] for _ in range(2)]
    for c in range(CH // 8):
        fields = [s["vec"][m, c * 8 : c * 8 + 8, :] for m in range(9)]
        for j in range(2):
            for level, tile in enumerate(project(ys[j], fields)):
                tiles[j][level].append(tile)
    proj = join(tiles)
    s["proj"][i] = proj
    high, low = split(s["mix"][i] * proj)
    x1h = s["x1"][i, 0:CH, :]
    x1l = s["x1"][i, CH : 2 * CH, :]
    z = dot(s["a4"][...], jnp.concatenate([x1h, high, x1l, low, x1h, high], axis=0))
    act, dact = silu_pair(z)
    wout = s["wout"][...]
    for j in range(2):
        k = 2 * i + j
        lanes = slice(j * SLOTS, (j + 1) * SLOTS)
        rows = pl.ds(pl.multiple_of((k * PART + G_EPS) * 8, 8), 8)
        s["part"][rows, :] = s["part"][rows, :] + tile_sum(act[:, lanes] * wout)
    gout = jnp.concatenate([wout * tall(row(s, 2 * i + j, ENV), 8) for j in range(2)], axis=1)
    gj = dot(s["a5"][...], stack3(gout * dact))
    s["gx1"][i] = gout + gj[:CH]
    gs = gj[CH:]
    ga_high, ga_low = split(gs * s["proj"][i])
    s["ga"][i, 0 : 3 * CH, :] = ga_high
    s["ga"][i, 3 * CH : 6 * CH, :] = ga_low
    s["q"][i] = gs * s["mix"][i]


def backward(i, s):
    ys = [harmonics_of(s, 2 * i + j) for j in range(2)]
    tiles = [[], []]
    turns = [[None] * 9 for _ in range(2)]
    for c in range(CH // 8):
        chan = slice(c * 8, c * 8 + 8)
        gfields = [s["gvec"][m, chan, :] for m in range(9)]
        fields = [None] + [s["vec"][m, chan, :] for m in range(1, 9)]
        for j in range(2):
            lanes = slice(j * SLOTS, (j + 1) * SLOTS)
            flow = s["gx1"][i, chan, lanes] + gfields[0]
            qs = [s["q"][i, l * CH + c * 8 : l * CH + c * 8 + 8, lanes] for l in range(3)]
            x1 = s["x1f"][i, chan, lanes]
            for m in range(1, 9):
                flow = flow + ys[j][m] * gfields[m]
                both = qs[LEVEL[m]] * fields[m] + x1 * gfields[m]
                turns[j][m] = both if c == 0 else turns[j][m] + both
            tiles[j].append(flow)
    for j in range(2):
        for m in range(1, 9):
            keep(s, 2 * i + j, G_HARM + m - 1, turns[j][m])
    flow = jnp.concatenate([jnp.concatenate(side, axis=0) for side in tiles], axis=1)
    ga_high = s["ga"][i, 0 : 3 * CH, :]
    ga_low = s["ga"][i, 3 * CH : 6 * CH, :]
    gx1 = flow + dot(s["a6"][...], jnp.concatenate([ga_high, ga_low, ga_high], axis=0))
    genv = tile_sum(gx1 * s["s2"][i])
    gh = dot(s["a7"][...], stack3(gx1 * s["d2"][i]))
    gb = dot(s["a8"][...], stack3(gh * s["dh"][i]))
    for j in range(2):
        k = 2 * i + j
        lanes = slice(j * SLOTS, (j + 1) * SLOTS)
        keep(s, k, G_ENV, genv[:, lanes])
        keep(s, k, G_RAD, gb[:, lanes] * s["dbas"][k])


def edge_forces(nbr, s):
    total = [jnp.zeros((8, SLOTS), F32) for _ in range(4)]
    for tile in range(4):
        rows = pl.ds(tile * 8, 8)
        valid = nbr[rows, :] >= 0
        ux, uy, uz, inv, denv, env = (s["dense"][r, rows, :] for r in range(6))

        def whole(r):
            terms = [
                s["part"][pl.ds((tile * 8 * PART + r) * 8 + lane, 8, stride=8 * PART), :]
                for lane in range(8)
            ]
            while len(terms) > 1:
                terms = [a + b for a, b in zip(terms[::2], terms[1::2])]
            return terms[0]

        y = [None] + [whole(G_HARM + m - 1) for m in range(1, 9)]
        eps = whole(G_EPS)
        gx = ROOT3 * y[1] + ROOT15 * (uy * y[4] + uz * y[7] + ux * y[8])
        gy = ROOT3 * y[2] + ROOT15 * (ux * y[4] + uz * y[5] - uy * y[8])
        gz = ROOT3 * y[3] + ROOT15 * (uy * y[5] + ux * y[7]) + (3.0 * ROOT5) * (uz * y[6])
        along = ux * gx + uy * gy + uz * gz
        radial = whole(G_RAD) + (whole(G_ENV) + eps) * denv - along * inv
        for c, (unit, g) in enumerate(((ux, gx), (uy, gy), (uz, gz))):
            value = jnp.where(valid, radial * unit + g * inv, 0.0)
            s["gr"][pl.ds(tile * 64 + c, 8, stride=8), :] = value
            total[c] = total[c] + value
        total[3] = total[3] + jnp.where(valid, eps * env, 0.0)
    return [jnp.sum(t, axis=0, keepdims=True) for t in total]


def scatter(i, total, nbr, s):
    lhs, rhs = [], []
    for j in range(2):
        k = 2 * i + j
        safe = jnp.maximum(nbr[pl.ds(k, 1), :], 0)
        here = lax.broadcasted_iota(jnp.int32, (32, SLOTS), 0) == (safe >> 7)
        rows = [
            jnp.where(here, jnp.broadcast_to(s["gr"][pl.ds(k * 8 + c, 1), :], (32, SLOTS)), 0.0)
            for c in range(3)
        ]
        lhs.append(jnp.concatenate(split(jnp.concatenate(rows, axis=0)), axis=0))
        slot = lax.broadcasted_iota(jnp.int32, (SLOTS, SLOTS), 0) == (safe & 127)
        rhs.append(jnp.where(slot, 1.0, 0.0).astype(BF16))
    return total + lax.dot_general(
        jnp.concatenate(lhs, axis=1),
        jnp.concatenate(rhs, axis=1),
        (((1,), (1,)), ((), ())),
        preferred_element_type=F32,
    )


def loop(body, unroll):
    blocks = PAIRS // unroll if unroll < PAIRS else 0

    def block(b, carry):
        for j in range(unroll):
            body(b * unroll + j)
        return carry

    if blocks:
        lax.fori_loop(0, blocks, block, 0)
    for i in range(blocks * unroll, PAIRS):
        body(i)


UNROLL = (13, 13, 13)


def compute(table, nbr, pos, spec, s):
    geometry(table, nbr, pos, s)
    order = lax.broadcasted_iota(jnp.int32, (8, SLOTS), 0)
    center_hot = jnp.where(spec == order, 1.0, 0.0)
    loop(lambda i: two_body(i, s, center_hot), UNROLL[0])
    accumulate(s["x1f"], 0, s, s["sums"])
    mix_levels(s["ae"], s["sums"], s["vec"])
    loop(lambda i: three_body(i, s), UNROLL[1])
    accumulate(s["q"], CH, s, s["sums"])
    mix_levels(s["ag"], s["sums"], s["gvec"])
    loop(lambda i: backward(i, s), UNROLL[2])
    center = edge_forces(nbr, s)
    spread = jnp.zeros((192, SLOTS), F32)
    for i in range(PAIRS):
        spread = scatter(i, spread, nbr, s)
    return center[3], center[:3], spread[:96] + spread[96:]


WEIGHTS = ("emb_center", "emb_neigh", "w_radial", "w_two", "w_pair", "w_latent", "w_out")
WIDE = 2 * SLOTS
SCRATCH = {
    "a1": ((CH, 64), BF16),
    "a2": ((CH, 192), BF16),
    "a3": ((3 * CH, 192), BF16),
    "a4": ((CH, 768), BF16),
    "a5": ((4 * CH, 192), BF16),
    "a6": ((CH, 576), BF16),
    "ae": ((3, CH, 192), BF16),
    "ag": ((3, CH, 192), BF16),
    "sums": ((CH, 9 * SLOTS), F32),
    "x1f": ((PAIRS, CH, WIDE), F32),
    "proj": ((PAIRS, 3 * CH, WIDE), F32),
    "a7": ((CH, 192), BF16),
    "a8": ((8, 192), BF16),
    "wout": ((CH, SLOTS), F32),
    "geo": ((32 * GEO, SLOTS), F32),
    "dense": ((6, 32, SLOTS), F32),
    "dbas": ((LIST, 8, SLOTS), F32),
    "dh": ((PAIRS, CH, WIDE), F32),
    "s2": ((PAIRS, CH, WIDE), F32),
    "d2": ((PAIRS, CH, WIDE), F32),
    "x1": ((PAIRS, 2 * CH, WIDE), BF16),
    "mix": ((PAIRS, 3 * CH, WIDE), F32),
    "vec": ((9, CH, SLOTS), F32),
    "gvec": ((9, CH, SLOTS), F32),
    "gx1": ((PAIRS, CH, WIDE), F32),
    "ga": ((PAIRS, 6 * CH, WIDE), BF16),
    "q": ((PAIRS, 3 * CH, WIDE), F32),
    "part": ((32 * PART * 8, SLOTS), F32),
    "gr": ((32 * 8, SLOTS), F32),
    "nbr": ((32, SLOTS), jnp.int32),
}


def neighbour(shift, sizes):
    return tuple(
        lax.rem(lax.axis_index(axis) + (d + size), size)
        for (axis, size), d in zip(sizes, shift)
    )


FAR_FIRST = sorted(OTHERS, key=lambda n: -sum(w * abs(d) for w, d in zip((2, 1, 2), SHIFTS[n])))


def kernel(sizes, *refs):
    pos_in, spec_in, nbr_in = refs[:3]
    weights = dict(zip(WEIGHTS, refs[3:10]))
    energy_out, force_out = refs[10:12]
    scratch = dict(zip(SCRATCH, refs[12 : 12 + len(SCRATCH)]))
    packed, table, outbox, inbox, send, recv, send_back, recv_back, list_sem = refs[
        12 + len(SCRATCH) :
    ]

    def remote(src, dst, sems, n):
        return pltpu.make_async_remote_copy(
            src_ref=src,
            dst_ref=dst,
            send_sem=sems[0],
            recv_sem=sems[1],
            device_id=neighbour(SHIFTS[n], sizes),
            device_id_type=MESH,
        )

    barrier = pltpu.get_barrier_semaphore()
    for n in FAR_FIRST:
        pl.semaphore_signal(
            barrier, inc=1, device_id=neighbour(SHIFTS[n], sizes), device_id_type=MESH
        )
    listing = pltpu.make_async_copy(
        nbr_in.at[0, 0, :, 0, :], scratch["nbr"].at[0:LIST, :], list_sem
    )
    scratch["nbr"][LIST:, :] = jnp.full((32 - LIST, SLOTS), -1, jnp.int32)
    listing.start()
    pos = pos_in[:, 0, 0, 0, :]
    spec = spec_in[0, 0]
    mine = jnp.concatenate([pos, spec.astype(F32)], axis=0)
    packed[...] = mine
    table[26] = mine
    prepare_weights(weights, scratch)
    listing.wait()
    pl.semaphore_wait(barrier, 26)

    for n in FAR_FIRST:
        remote(packed, table.at[PLACE[26 - n]], (send, recv), n).start()
    everyone = table.at[0:26]
    remote(everyone, everyone, (send, recv), 0).wait()

    energy, center, spread = compute(table, scratch["nbr"], pos, spec, scratch)
    energy_out[0, 0] = energy
    for c in range(3):
        outbox[:, c, :] = spread[c * 32 : (c + 1) * 32]
    for n in FAR_FIRST:
        remote(outbox.at[n], inbox.at[PLACE[26 - n]], (send_back, recv_back), n).start()
    force = jnp.concatenate(center, axis=0) - outbox[13, 0:3, :]
    everyone = inbox.at[0:26]
    remote(everyone, everyone, (send_back, recv_back), 0).wait()
    for place in range(26):
        force = force - inbox[place, 0:3, :]
    force_out[:, 0, 0, 0, :] = force


def solution(mesh):
    sizes = tuple((axis, mesh.shape[axis]) for axis in ("gx", "gy", "gz"))

    def local(positions, species, neighbours, emb_c, emb_n, w_rad, w_two, w_pair, w_lat, w_out):
        vmem = pl.BlockSpec(memory_space=pltpu.VMEM)
        dma = pltpu.SemaphoreType.DMA
        return pl.pallas_call(
            functools.partial(kernel, sizes),
            out_shape=(
                pltpu.VMEM(species.shape, F32),
                pltpu.VMEM(positions.shape, F32),
            ),
            in_specs=[vmem] * 2 + [pl.BlockSpec(memory_space=pl.ANY)] + [vmem] * 7,
            out_specs=(vmem, vmem),
            scratch_shapes=[pltpu.VMEM(*spec) for spec in SCRATCH.values()]
            + [
                pltpu.VMEM((4, SLOTS), F32),
                pltpu.VMEM((27, 4, SLOTS), F32),
                pltpu.VMEM((32, 8, SLOTS), F32),
                pltpu.VMEM((26, 8, SLOTS), F32),
            ]
            + [dma] * 5,
            compiler_params=pltpu.CompilerParams(
                collective_id=0, has_side_effects=True, vmem_limit_bytes=60 << 20
            ),
        )(
            positions, species, jnp.swapaxes(neighbours, 2, 3), emb_c, emb_n, w_rad, w_two, w_pair,
            w_lat.T, w_out.reshape(1, CH),
        )

    placed = (
        P(None, "gx", "gy", "gz", None),
        P("gx", "gy", "gz", None),
        P("gx", "gy", "gz", None, None),
    ) + (P(),) * 7
    return jax.shard_map(
        local,
        mesh=mesh,
        in_specs=placed,
        out_specs=(P("gx", "gy", "gz", None), P(None, "gx", "gy", "gz", None)),
        check_vma=False,
    )
```

```python
import functools
import math

import jax
import jax.numpy as jnp
from jax import lax
from jax.experimental import pallas as pl
from jax.experimental.pallas import tpu as pltpu
from jax.sharding import PartitionSpec as P

MESH = pl.DeviceIdType.MESH
F32 = jnp.float32
BF16 = jnp.bfloat16
RADIUS = 5.0
EDGES = (8.6, 8.6, 17.2)
SCALE = 0.125
CH = 64
SLOTS = 128
LIST = 26
PAIRS = LIST // 2
NSPEC = 5
LEVEL = (0, 1, 1, 1, 2, 2, 2, 2, 2)
SHIFTS = tuple((x, y, z) for x in (-1, 0, 1) for y in (-1, 0, 1) for z in (-1, 0, 1))
OTHERS = [n for n in range(27) if n != 13]
PLACE = {n: place for place, n in enumerate(OTHERS)} | {13: 26}
XS, INVD, ENV, KIND, HARM = 0, 1, 2, 3, 4
G_RAD, G_ENV, G_EPS, G_HARM = 0, 1, 2, 3
GEO, PART = 16, 11
BLOCK = 16
ROOT3, ROOT5, ROOT15 = math.sqrt(3.0), math.sqrt(5.0), math.sqrt(15.0)


def split(x):
    high = x.astype(BF16)
    low = (x - high.astype(F32)).astype(BF16)
    return high, low


def stack3(x):
    high, low = split(x)
    return jnp.concatenate([high, low, high], axis=0)


def dot(lhs, rhs):
    return jnp.dot(lhs, rhs, preferred_element_type=F32)


def tall_dot(weights, high, low):
    both = dot(weights[...], high)
    rows = both.shape[0] // 2
    return both[:rows] + both[rows:] + dot(weights[0:rows, :], low)


def silu_pair(half):
    turn = jnp.tanh(half)
    act = half + half * turn
    return act, act - act * turn + turn + 1.0


def transpose_stack(w):
    high = w.astype(BF16).astype(F32)
    return jnp.concatenate([high, high, w - high], axis=0).T.astype(BF16)


def prepare_weights(w, s):
    zero = lambda rows: jnp.zeros((rows, CH), F32)
    parts = []
    radial = w["w_radial"][...]
    rh = radial.astype(BF16).astype(F32)
    parts += [rh, rh, radial - rh]
    for name in ("emb_neigh", "emb_center"):
        emb = w[name][...]
        eh = emb.astype(BF16).astype(F32)
        parts += [jnp.concatenate([eh, zero(8 - NSPEC)], axis=0)]
        parts += [jnp.concatenate([emb - eh, zero(8 - NSPEC)], axis=0)]
    parts += [zero(8)]
    s["a1"][...] = (0.5 * jnp.concatenate(parts, axis=0)).T.astype(BF16)
    two = w["w_two"][...]
    s["a2"][...] = transpose_stack(0.5 * two)
    s["a7"][...] = transpose_stack(0.5 * two.T)
    s["a8"][...] = transpose_stack(0.5 * radial.T)
    pair = w["w_pair"][...]
    s["a3"][...] = transpose_stack(pair[:, 3 * CH :])
    turned = pair.T
    s["a6"][...] = jnp.concatenate(split(pair[:, 3 * CH :]), axis=0)
    for level in range(3):
        s["ae"][level] = transpose_stack(SCALE * pair[:, level * CH : (level + 1) * CH])
        s["ag"][level] = transpose_stack(SCALE * turned[level * CH : (level + 1) * CH])
    latent = w["w_latent"][...]
    s["a4"][...] = jnp.concatenate(split(0.5 * latent), axis=0)
    s["a5"][...] = transpose_stack(0.5 * latent)
    s["wout"][...] = jnp.broadcast_to(w["w_out"][...].T, (CH, SLOTS))


def geometry(table, nbr, pos, s):
    for tile in range(4):
        rows = pl.ds(tile * 8, 8)
        index = nbr[rows, :]
        valid = index >= 0
        safe = jnp.maximum(index, 0)
        code = safe >> 7
        slot = safe & 127
        got = [jnp.zeros((8, SLOTS), F32) for _ in range(4)]
        for n, shift in enumerate(SHIFTS):
            here = code == n
            for c in range(4):
                source = jnp.broadcast_to(table[PLACE[n], c : c + 1, :], (8, SLOTS))
                value = jnp.take_along_axis(source, slot, axis=1, mode="promise_in_bounds")
                if c < 3 and shift[c]:
                    value = value + shift[c] * EDGES[c]
                got[c] = jnp.where(here, value, got[c])
        delta = [jnp.where(valid, got[c] - pos[c : c + 1, :], 1.0) for c in range(3)]
        square = delta[0] * delta[0] + delta[1] * delta[1] + delta[2] * delta[2]
        dist = jnp.sqrt(square)
        inv = 1.0 / dist
        ux, uy, uz = (d * inv for d in delta)
        scaled = dist * (1.0 / RADIUS)
        inside = jnp.logical_and(valid, scaled < 1.0)
        sq = scaled * scaled
        p5 = sq * sq * scaled
        p6 = p5 * scaled
        env = 1.0 + p6 * (-28.0 + scaled * (48.0 - 21.0 * scaled))
        denv = (1.0 / RADIUS) * p5 * (-168.0 + scaled * (336.0 - 168.0 * scaled))
        env = jnp.where(inside, env, 0.0)
        denv = jnp.where(inside, denv, 0.0)
        values = [jnp.minimum(scaled, 1.0), inv, env, got[3]]
        values += [ROOT3 * ux, ROOT3 * uy, ROOT3 * uz, ROOT15 * ux * uy, ROOT15 * uy * uz]
        values += [0.5 * ROOT5 * (3.0 * uz * uz - 1.0), ROOT15 * ux * uz]
        values += [0.5 * ROOT15 * (ux * ux - uy * uy)]
        for r, v in enumerate(values):
            s["geo"][pl.ds(tile * 8 * GEO + r, 8, stride=GEO), :] = v
        for r, v in enumerate((ux, uy, uz, inv, denv, env)):
            s["dense"][r, rows, :] = v


def row(s, k, r):
    return jnp.broadcast_to(s["geo"][pl.ds(k * GEO + r, 1), :], (8, SLOTS))


def tile_sum(x):
    return jnp.sum(x.reshape(x.shape[0] // 8, 8, x.shape[1]), axis=0)


def tall(tile, count):
    return jnp.concatenate([tile] * count, axis=0)


def keep(s, k, r, tile):
    start = (k * PART + r) * 8
    s["part"][pl.ds(start if isinstance(start, int) else pl.multiple_of(start, 8), 8), :] = tile


def two_body(i, s, center_hot):
    order = lax.broadcasted_iota(jnp.int32, (8, SLOTS), 0).astype(F32)
    columns = []
    for j in range(2):
        k = 2 * i + j
        turns = (order + 1.0) * row(s, k, XS)
        inv = row(s, k, INVD)
        whole = jnp.floor(turns + 0.5)
        part = turns - whole
        odd = whole - 2.0 * jnp.floor(0.5 * whole)
        sign = (1.0 - 2.0 * odd) * (math.sqrt(2.0 / RADIUS) * inv)
        sine, cosine = sincospi(part)
        basis = sign * sine
        s["dbas"][k] = (sign * cosine) * ((order + 1.0) * (math.pi / RADIUS)) - basis * inv
        hot = jnp.where(row(s, k, KIND) == order, 1.0, 0.0)
        high = basis.astype(BF16).astype(F32)
        zero = jnp.zeros((8, SLOTS), F32)
        columns.append(
            jnp.concatenate(
                [high, basis - high, high, hot, hot, center_hot, center_hot, zero], axis=0
            ).astype(BF16)
        )
    columns = jnp.concatenate(columns, axis=1)
    yield
    act, dact = silu_pair(dot(s["a1"][...], columns))
    s["dh"][i] = dact
    act = stack3(act)
    yield
    act2, dact2 = silu_pair(dot(s["a2"][...], act))
    env = jnp.concatenate([tall(row(s, 2 * i + j, ENV), 8) for j in range(2)], axis=1)
    s["s2"][i] = act2
    s["d2"][i] = dact2 * env
    x1 = act2 * env
    for j in range(2):
        lanes = slice(j * SLOTS, (j + 1) * SLOTS)
        keep(s, 2 * i + j, G_EPS, tile_sum(x1[:, lanes] * s["wout"][...]))
    high, low = split(x1)
    s["x1f"][i] = x1
    s["x1"][i, 0:CH, :] = high
    s["x1"][i, CH : 2 * CH, :] = low
    yield
    s["mix"][i] = dot(s["a3"][...], jnp.concatenate([high, low, high], axis=0))


def sincospi(part):
    t = part * math.pi
    q = t * t
    sine = 1.0 / 6227020800.0
    for c in (-1.0 / 39916800, 1.0 / 362880, -1.0 / 5040, 1.0 / 120, -1.0 / 6):
        sine = sine * q + c
    sine = t + t * (q * sine)
    cosine = -1.0 / 87178291200.0
    for c in (1.0 / 479001600, -1.0 / 3628800, 1.0 / 40320, -1.0 / 720, 1.0 / 24, -0.5, 1.0):
        cosine = cosine * q + c
    return sine, cosine


def accumulate(source, level_rows, s, target):
    for chan in range(0, CH, BLOCK):
        total = [None] * 9
        for i in range(PAIRS):
            for j in range(2):
                lanes = slice(j * SLOTS, (j + 1) * SLOTS)
                starts = [l * level_rows + chan for l in range(3 if level_rows else 1)]
                parts = [source[i, a : a + BLOCK, lanes] for a in starts]
                for m in range(9):
                    part = parts[LEVEL[m] if level_rows else 0]
                    if m:
                        part = part * tall(row(s, 2 * i + j, HARM + m - 1), BLOCK // 8)
                    total[m] = part if total[m] is None else total[m] + part
        for m in range(9):
            target[chan : chan + BLOCK, m * SLOTS : (m + 1) * SLOTS] = total[m]


def mix_levels(weights, source, target):
    for level, (low, high) in enumerate(((0, 1), (1, 4), (4, 9))):
        lanes = slice(low * SLOTS, high * SLOTS)
        mixed = dot(weights[level], stack3(source[:, lanes]))
        for m in range(low, high):
            target[m] = mixed[:, (m - low) * SLOTS : (m - low + 1) * SLOTS]


def project(ys, fields):
    out = [fields[0], None, None]
    for m in range(1, 9):
        term = ys[m] * fields[m]
        level = LEVEL[m]
        out[level] = term if out[level] is None else out[level] + term
    return out


def harmonics_of(s, k):
    return [None] + [row(s, k, HARM + m - 1) for m in range(1, 9)]


def tensors(i, s):
    for j in range(2):
        lanes = slice(j * SLOTS, (j + 1) * SLOTS)
        ys = harmonics_of(s, 2 * i + j)
        for c in range(0, CH, 16):
            tiles = [[], [], []]
            for chan in (c, c + 8):
                fields = [s["vec"][m, chan : chan + 8, :] for m in range(9)]
                for level, tile in enumerate(project(ys, fields)):
                    tiles[level].append(tile)
            for level in range(3):
                proj = jnp.concatenate(tiles[level], axis=0)
                at = level * CH + c
                s["proj"][i, at : at + 16, lanes] = proj
                high, low = split(s["mix"][i, at : at + 16, lanes] * proj)
                s["scal"][i, at : at + 16, lanes] = high
                s["scal"][i, 3 * CH + at : 3 * CH + at + 16, lanes] = low


def three_body(i, s):
    high = s["scal"][i, 0 : 3 * CH, :]
    low = s["scal"][i, 3 * CH : 6 * CH, :]
    x1h = s["x1"][i, 0:CH, :]
    x1l = s["x1"][i, CH : 2 * CH, :]
    z = tall_dot(
        s["a4"], jnp.concatenate([x1h, high], axis=0), jnp.concatenate([x1l, low], axis=0)
    )
    act, dact = silu_pair(z)
    wout = s["wout"][...]
    for j in range(2):
        k = 2 * i + j
        lanes = slice(j * SLOTS, (j + 1) * SLOTS)
        rows = pl.ds((k * PART + G_EPS) * 8, 8)
        s["part"][rows, :] = s["part"][rows, :] + tile_sum(act[:, lanes] * wout)
    gout = jnp.concatenate([wout * tall(row(s, 2 * i + j, ENV), 8) for j in range(2)], axis=1)
    gz = stack3(gout * dact)
    yield
    gj = dot(s["a5"][...], gz)
    s["gx1"][i] = gout + gj[:CH]
    gs = gj[CH:]
    s["q"][i] = gs * s["mix"][i]
    high, low = split(gs * s["proj"][i])
    yield
    s["gx1"][i] = s["gx1"][i] + tall_dot(s["a6"], high, low)


def flows(i, s):
    for j in range(2):
        k = 2 * i + j
        lanes = slice(j * SLOTS, (j + 1) * SLOTS)
        ys = harmonics_of(s, k)
        turns = [None] * 9
        for c in range(0, CH, 8):
            chan = slice(c, c + 8)
            qs = [s["q"][i, l * CH + c : l * CH + c + 8, lanes] for l in range(3)]
            x1 = s["x1f"][i, chan, lanes]
            flow = s["gx1"][i, chan, lanes] + s["gvec"][0, chan, :]
            for m in range(1, 9):
                gfield = s["gvec"][m, chan, :]
                flow = flow + ys[m] * gfield
                both = qs[LEVEL[m]] * s["vec"][m, chan, :] + x1 * gfield
                turns[m] = both if c == 0 else turns[m] + both
            s["gx1"][i, chan, lanes] = flow
        for m in range(1, 9):
            keep(s, k, G_HARM + m - 1, turns[m])


def backward(i, s):
    gx1 = s["gx1"][i]
    genv = tile_sum(gx1 * s["s2"][i])
    gh = stack3(gx1 * s["d2"][i])
    yield
    gh = stack3(dot(s["a7"][...], gh) * s["dh"][i])
    yield
    gb = dot(s["a8"][...], gh)
    for j in range(2):
        k = 2 * i + j
        lanes = slice(j * SLOTS, (j + 1) * SLOTS)
        keep(s, k, G_ENV, genv[:, lanes])
        keep(s, k, G_RAD, gb[:, lanes] * s["dbas"][k])


def edge_forces(nbr, s):
    total = [jnp.zeros((8, SLOTS), F32) for _ in range(4)]
    for tile in range(4):
        rows = pl.ds(tile * 8, 8)
        valid = nbr[rows, :] >= 0
        ux, uy, uz, inv, denv, env = (s["dense"][r, rows, :] for r in range(6))

        def whole(r):
            terms = [
                s["part"][pl.ds((tile * 8 * PART + r) * 8 + lane, 8, stride=8 * PART), :]
                for lane in range(8)
            ]
            while len(terms) > 1:
                terms = [a + b for a, b in zip(terms[::2], terms[1::2])]
            return terms[0]

        y = [None] + [whole(G_HARM + m - 1) for m in range(1, 9)]
        eps = whole(G_EPS)
        gx = ROOT3 * y[1] + ROOT15 * (uy * y[4] + uz * y[7] + ux * y[8])
        gy = ROOT3 * y[2] + ROOT15 * (ux * y[4] + uz * y[5] - uy * y[8])
        gz = ROOT3 * y[3] + ROOT15 * (uy * y[5] + ux * y[7]) + (3.0 * ROOT5) * (uz * y[6])
        along = ux * gx + uy * gy + uz * gz
        radial = whole(G_RAD) + (whole(G_ENV) + eps) * denv - along * inv
        for c, (unit, g) in enumerate(((ux, gx), (uy, gy), (uz, gz))):
            value = jnp.where(valid, radial * unit + g * inv, 0.0)
            high = value.astype(BF16).astype(F32)
            s["gr"][pl.ds(tile * 64 + c, 8, stride=8), :] = high
            s["gr"][pl.ds(tile * 64 + 3 + c, 8, stride=8), :] = value - high
            total[c] = total[c] + value
        total[3] = total[3] + jnp.where(valid, eps * env, 0.0)
    return [jnp.sum(t, axis=0, keepdims=True) for t in total]


def prepare_scatter(i, nbr, s):
    for j in range(2):
        k = 2 * i + j
        safe = jnp.maximum(nbr[pl.ds(k, 1), :], 0)
        here = lax.broadcasted_iota(jnp.int32, (32, SLOTS), 0) == (safe >> 7)
        s["codes"][k] = jnp.where(here, 1.0, 0.0)
        slot = lax.broadcasted_iota(jnp.int32, (SLOTS, SLOTS), 0) == (safe & 127)
        lanes = pl.ds(pl.multiple_of(k * SLOTS, SLOTS), SLOTS)
        s["hot"][:, lanes] = jnp.where(slot, 1.0, 0.0).astype(BF16)


def scatter(s):
    for k in range(LIST):
        codes = s["codes"][k]
        rows = [s["gr"][k * 8 + c : k * 8 + c + 1, :] for c in range(6)]
        lanes = slice(k * SLOTS, (k + 1) * SLOTS)
        s["sent"][:, lanes] = jnp.concatenate([codes * r for r in rows], axis=0).astype(BF16)
    return lax.dot_general(
        s["sent"][...], s["hot"][...], (((1,), (1,)), ((), ())), preferred_element_type=F32
    )


def loop(body):
    lax.fori_loop(0, PAIRS, lambda i, carry: (body(i), carry)[1], 0)


def lockstep(body, group):
    for start in range(0, PAIRS, group):
        live = [body(i) for i in range(start, min(start + group, PAIRS))]
        while live:
            live = [stage for stage in live if next(stage, True) is None]


GROUPS = (13, 7, 13)


def compute(table, nbr, pos, spec, s):
    geometry(table, nbr, pos, s)
    order = lax.broadcasted_iota(jnp.int32, (8, SLOTS), 0)
    center_hot = jnp.where(spec == order, 1.0, 0.0)
    lockstep(lambda i: two_body(i, s, center_hot), GROUPS[0])
    accumulate(s["x1f"], 0, s, s["sums"])
    mix_levels(s["ae"], s["sums"], s["vec"])
    loop(lambda i: tensors(i, s))
    lockstep(lambda i: three_body(i, s), GROUPS[1])
    accumulate(s["q"], CH, s, s["sums"])
    mix_levels(s["ag"], s["sums"], s["gvec"])
    loop(lambda i: flows(i, s))
    lockstep(lambda i: backward(i, s), GROUPS[2])
    center = edge_forces(nbr, s)
    spread = scatter(s)
    return center[3], center[:3], spread[:96] + spread[96:]


WEIGHTS = ("emb_center", "emb_neigh", "w_radial", "w_two", "w_pair", "w_latent", "w_out")
WIDE = 2 * SLOTS
SCRATCH = {
    "a1": ((CH, 64), BF16),
    "a2": ((CH, 192), BF16),
    "a3": ((3 * CH, 192), BF16),
    "a4": ((2 * CH, 256), BF16),
    "a5": ((4 * CH, 192), BF16),
    "a6": ((2 * CH, 192), BF16),
    "ae": ((3, CH, 192), BF16),
    "ag": ((3, CH, 192), BF16),
    "sums": ((CH, 9 * SLOTS), F32),
    "x1f": ((PAIRS, CH, WIDE), F32),
    "proj": ((PAIRS, 3 * CH, WIDE), F32),
    "a7": ((CH, 192), BF16),
    "a8": ((8, 192), BF16),
    "wout": ((CH, SLOTS), F32),
    "geo": ((32 * GEO, SLOTS), F32),
    "dense": ((6, 32, SLOTS), F32),
    "dbas": ((LIST, 8, SLOTS), F32),
    "dh": ((PAIRS, CH, WIDE), F32),
    "s2": ((PAIRS, CH, WIDE), F32),
    "d2": ((PAIRS, CH, WIDE), F32),
    "x1": ((PAIRS, 2 * CH, WIDE), BF16),
    "mix": ((PAIRS, 3 * CH, WIDE), F32),
    "vec": ((9, CH, SLOTS), F32),
    "gvec": ((9, CH, SLOTS), F32),
    "gx1": ((PAIRS, CH, WIDE), F32),
    "scal": ((PAIRS, 6 * CH, WIDE), BF16),
    "sent": ((192, LIST * SLOTS), BF16),
    "q": ((PAIRS, 3 * CH, WIDE), F32),
    "part": ((32 * PART * 8, SLOTS), F32),
    "gr": ((32 * 8, SLOTS), F32),
    "nbr": ((32, SLOTS), jnp.int32),
    "codes": ((LIST, 32, SLOTS), F32),
    "hot": ((SLOTS, LIST * SLOTS), BF16),
}


def neighbour(shift, sizes):
    return tuple(
        lax.rem(lax.axis_index(axis) + (d + size), size)
        for (axis, size), d in zip(sizes, shift)
    )


FAR_FIRST = sorted(OTHERS, key=lambda n: -sum(w * abs(d) for w, d in zip((2, 1, 2), SHIFTS[n])))


def total_of(terms):
    while len(terms) > 1:
        terms = [sum(terms[i : i + 2][1:], terms[i]) for i in range(0, len(terms), 2)]
    return terms[0]


def kernel(sizes, *refs):
    inputs = refs[:10]
    energy_out, force_out = refs[10:12]
    scratch = dict(zip(SCRATCH, refs[12 : 12 + len(SCRATCH)]))
    refs = refs[12 + len(SCRATCH) :]
    copied, weights = refs[:7], dict(zip(WEIGHTS, refs[:7]))
    packed, table, outbox, inbox, spec_ref, send, recv, send_back, recv_back, sems = refs[7:]
    nbr = scratch["nbr"]

    def remote(src, dst, pair, n):
        return pltpu.make_async_remote_copy(
            src_ref=src,
            dst_ref=dst,
            send_sem=pair[0],
            recv_sem=pair[1],
            device_id=neighbour(SHIFTS[n], sizes),
            device_id_type=MESH,
        )

    own = [
        pltpu.make_async_copy(inputs[1].at[0, 0], spec_ref, sems.at[0]),
        pltpu.make_async_copy(inputs[0].at[:, 0, 0, 0, :], packed.at[0:3], sems.at[1]),
        pltpu.make_async_copy(inputs[2].at[0, 0, :, 0, :], nbr.at[0:LIST, :], sems.at[2]),
    ]
    own += [
        pltpu.make_async_copy(src, dst, sems.at[3 + i])
        for i, (src, dst) in enumerate(zip(inputs[3:], copied))
    ]
    own[0].start()
    own[1].start()
    barrier = pltpu.get_barrier_semaphore()
    for n in FAR_FIRST:
        pl.semaphore_signal(
            barrier, inc=1, device_id=neighbour(SHIFTS[n], sizes), device_id_type=MESH
        )
    for copy in own[2:]:
        copy.start()
    nbr[LIST:, :] = jnp.full((32 - LIST, SLOTS), -1, jnp.int32)
    outbox[:, 3, :] = jnp.zeros((32, SLOTS), F32)
    own[0].wait()
    spec = spec_ref[...]
    packed[3:4, :] = spec.astype(F32)
    own[1].wait()
    pl.semaphore_wait(barrier, 26)

    for n in FAR_FIRST:
        remote(packed, table.at[PLACE[26 - n]], (send, recv), n).start()
    table[26] = packed[...]
    pos = packed[0:3, :]
    for copy in own[2:]:
        copy.wait()
    prepare_weights(weights, scratch)
    loop(lambda i: prepare_scatter(i, nbr, scratch))
    everyone = table.at[0:26]
    remote(everyone, everyone, (send, recv), 0).wait()

    energy, center, spread = compute(table, nbr, pos, spec, scratch)
    for c in range(3):
        outbox[:, c, :] = spread[c * 32 : (c + 1) * 32]
    for n in FAR_FIRST:
        remote(outbox.at[n], inbox.at[PLACE[26 - n]], (send_back, recv_back), n).start()
    energy_out[0, 0] = energy
    force = jnp.concatenate(center, axis=0) - outbox[13, 0:3, :]
    everyone = inbox.at[0:26]
    remote(everyone, everyone, (send_back, recv_back), 0).wait()
    force_out[:, 0, 0, 0, :] = force - total_of([inbox[i, 0:3, :] for i in range(26)])


def solution(mesh):
    sizes = tuple((axis, mesh.shape[axis]) for axis in ("gx", "gy", "gz"))

    def local(positions, species, neighbours, emb_c, emb_n, w_rad, w_two, w_pair, w_lat, w_out):
        vmem = pl.BlockSpec(memory_space=pltpu.VMEM)
        dma = pltpu.SemaphoreType.DMA
        weights = (emb_c, emb_n, w_rad, w_two, w_pair, w_lat.T, w_out.reshape(1, CH))
        return pl.pallas_call(
            functools.partial(kernel, sizes),
            out_shape=(
                pltpu.VMEM(species.shape, F32),
                pltpu.VMEM(positions.shape, F32),
            ),
            in_specs=[pl.BlockSpec(memory_space=pl.ANY)] * 10,
            out_specs=(vmem, vmem),
            scratch_shapes=[pltpu.VMEM(*spec) for spec in SCRATCH.values()]
            + [pltpu.VMEM(w.shape, F32) for w in weights]
            + [
                pltpu.VMEM((4, SLOTS), F32),
                pltpu.VMEM((27, 4, SLOTS), F32),
                pltpu.VMEM((32, 4, SLOTS), F32),
                pltpu.VMEM((26, 4, SLOTS), F32),
                pltpu.VMEM((1, SLOTS), jnp.int32),
            ]
            + [dma] * 4
            + [dma((10,))],
            compiler_params=pltpu.CompilerParams(
                collective_id=0, has_side_effects=True, vmem_limit_bytes=60 << 20
            ),
        )(positions, species, jnp.swapaxes(neighbours, 2, 3), *weights)

    placed = (
        P(None, "gx", "gy", "gz", None),
        P("gx", "gy", "gz", None),
        P("gx", "gy", "gz", None, None),
    ) + (P(),) * 7
    return jax.shard_map(
        local,
        mesh=mesh,
        in_specs=placed,
        out_specs=(P("gx", "gy", "gz", None), P(None, "gx", "gy", "gz", None)),
        check_vma=False,
    )
```

```python
import functools
import math

import jax
import jax.numpy as jnp
from jax import lax
from jax.experimental import pallas as pl
from jax.experimental.pallas import tpu as pltpu
from jax.sharding import PartitionSpec as P

MESH = pl.DeviceIdType.MESH
F32 = jnp.float32
BF16 = jnp.bfloat16
RADIUS = 5.0
EDGES = (8.6, 8.6, 17.2)
SCALE = 0.125
CH = 64
SLOTS = 128
LIST = 26
PAIRS = LIST // 2
NSPEC = 5
LEVEL = (0, 1, 1, 1, 2, 2, 2, 2, 2)
SHIFTS = tuple((x, y, z) for x in (-1, 0, 1) for y in (-1, 0, 1) for z in (-1, 0, 1))
OTHERS = [n for n in range(27) if n != 13]
PLACE = {n: place for place, n in enumerate(OTHERS)} | {13: 26}
XS, INVD, ENV, KIND, HARM = 0, 1, 2, 3, 4
G_RAD, G_ENV, G_EPS, G_HARM = 0, 1, 2, 3
GEO, PART = 16, 11
BLOCK = 16
ROOT3, ROOT5, ROOT15 = math.sqrt(3.0), math.sqrt(5.0), math.sqrt(15.0)


def split(x):
    high = x.astype(BF16)
    low = (x - high.astype(F32)).astype(BF16)
    return high, low


def stack3(x):
    high, low = split(x)
    return jnp.concatenate([high, low, high], axis=0)


def dot(lhs, rhs):
    return jnp.dot(lhs, rhs, preferred_element_type=F32)


def tall_dot(weights, high, low):
    both = dot(weights[...], high)
    rows = both.shape[0] // 2
    return both[:rows] + both[rows:] + dot(weights[0:rows, :], low)


def silu_pair(half):
    turn = jnp.tanh(half)
    act = half + half * turn
    return act, act - act * turn + turn + 1.0


def transpose_stack(w):
    high = w.astype(BF16).astype(F32)
    return jnp.concatenate([high, high, w - high], axis=0).T.astype(BF16)


def prepare_weights(w, s):
    zero = lambda rows: jnp.zeros((rows, CH), F32)
    parts = []
    radial = w["w_radial"][...]
    rh = radial.astype(BF16).astype(F32)
    parts += [rh, rh, radial - rh]
    for name in ("emb_neigh", "emb_center"):
        emb = w[name][...]
        eh = emb.astype(BF16).astype(F32)
        parts += [jnp.concatenate([eh, zero(8 - NSPEC)], axis=0)]
        parts += [jnp.concatenate([emb - eh, zero(8 - NSPEC)], axis=0)]
    parts += [zero(8)]
    s["a1"][...] = (0.5 * jnp.concatenate(parts, axis=0)).T.astype(BF16)
    two = w["w_two"][...]
    s["a2"][...] = transpose_stack(0.5 * two)
    s["a7"][...] = transpose_stack(0.5 * two.T)
    s["a8"][...] = transpose_stack(0.5 * radial.T)
    pair = w["w_pair"][...]
    s["a3"][...] = transpose_stack(pair[:, 3 * CH :])
    turned = pair.T
    s["a6"][...] = jnp.concatenate(split(pair[:, 3 * CH :]), axis=0)
    for level in range(3):
        s["ae"][level] = transpose_stack(SCALE * pair[:, level * CH : (level + 1) * CH])
        s["ag"][level] = transpose_stack(SCALE * turned[level * CH : (level + 1) * CH])
    latent = w["w_latent"][...]
    s["a4"][...] = jnp.concatenate(split(0.5 * latent), axis=0)
    s["a5"][...] = transpose_stack(0.5 * latent)
    s["wout"][...] = jnp.broadcast_to(w["w_out"][...].T, (CH, SLOTS))


def geometry(table, nbr, pos, s):
    for tile in range(4):
        rows = pl.ds(tile * 8, 8)
        index = nbr[rows, :]
        valid = index >= 0
        safe = jnp.maximum(index, 0)
        code = safe >> 7
        slot = safe & 127
        got = [jnp.zeros((8, SLOTS), F32) for _ in range(4)]
        for n, shift in enumerate(SHIFTS):
            here = code == n
            for c in range(4):
                source = jnp.broadcast_to(table[PLACE[n], c : c + 1, :], (8, SLOTS))
                value = jnp.take_along_axis(source, slot, axis=1, mode="promise_in_bounds")
                if c < 3 and shift[c]:
                    value = value + shift[c] * EDGES[c]
                got[c] = jnp.where(here, value, got[c])
        delta = [jnp.where(valid, got[c] - pos[c : c + 1, :], 1.0) for c in range(3)]
        square = delta[0] * delta[0] + delta[1] * delta[1] + delta[2] * delta[2]
        dist = jnp.sqrt(square)
        inv = 1.0 / dist
        ux, uy, uz = (d * inv for d in delta)
        scaled = dist * (1.0 / RADIUS)
        inside = jnp.logical_and(valid, scaled < 1.0)
        sq = scaled * scaled
        p5 = sq * sq * scaled
        p6 = p5 * scaled
        env = 1.0 + p6 * (-28.0 + scaled * (48.0 - 21.0 * scaled))
        denv = (1.0 / RADIUS) * p5 * (-168.0 + scaled * (336.0 - 168.0 * scaled))
        env = jnp.where(inside, env, 0.0)
        denv = jnp.where(inside, denv, 0.0)
        values = [jnp.minimum(scaled, 1.0), inv, env, got[3]]
        values += [ROOT3 * ux, ROOT3 * uy, ROOT3 * uz, ROOT15 * ux * uy, ROOT15 * uy * uz]
        values += [0.5 * ROOT5 * (3.0 * uz * uz - 1.0), ROOT15 * ux * uz]
        values += [0.5 * ROOT15 * (ux * ux - uy * uy)]
        for r, v in enumerate(values):
            s["geo"][pl.ds(tile * 8 * GEO + r, 8, stride=GEO), :] = v
        for r, v in enumerate((ux, uy, uz, inv, denv, env)):
            s["dense"][r, rows, :] = v


def row(s, k, r):
    return jnp.broadcast_to(s["geo"][pl.ds(k * GEO + r, 1), :], (8, SLOTS))


def tile_sum(x):
    return jnp.sum(x.reshape(x.shape[0] // 8, 8, x.shape[1]), axis=0)


def tall(tile, count):
    return jnp.concatenate([tile] * count, axis=0)


def keep(s, k, r, tile):
    start = (k * PART + r) * 8
    s["part"][pl.ds(start if isinstance(start, int) else pl.multiple_of(start, 8), 8), :] = tile


def two_body(i, s, center_hot):
    order = lax.broadcasted_iota(jnp.int32, (8, SLOTS), 0).astype(F32)
    columns = []
    for j in range(2):
        k = 2 * i + j
        turns = (order + 1.0) * row(s, k, XS)
        inv = row(s, k, INVD)
        whole = jnp.floor(turns + 0.5)
        part = turns - whole
        odd = whole - 2.0 * jnp.floor(0.5 * whole)
        sign = (1.0 - 2.0 * odd) * (math.sqrt(2.0 / RADIUS) * inv)
        sine, cosine = sincospi(part)
        basis = sign * sine
        s["dbas"][k] = (sign * cosine) * ((order + 1.0) * (math.pi / RADIUS)) - basis * inv
        hot = jnp.where(row(s, k, KIND) == order, 1.0, 0.0)
        high = basis.astype(BF16).astype(F32)
        zero = jnp.zeros((8, SLOTS), F32)
        columns.append(
            jnp.concatenate(
                [high, basis - high, high, hot, hot, center_hot, center_hot, zero], axis=0
            ).astype(BF16)
        )
    columns = jnp.concatenate(columns, axis=1)
    yield
    act, dact = silu_pair(dot(s["a1"][...], columns))
    s["dh"][i] = dact
    act = stack3(act)
    yield
    act2, dact2 = silu_pair(dot(s["a2"][...], act))
    env = jnp.concatenate([tall(row(s, 2 * i + j, ENV), 8) for j in range(2)], axis=1)
    s["s2"][i] = act2
    s["d2"][i] = dact2 * env
    x1 = act2 * env
    for j in range(2):
        lanes = slice(j * SLOTS, (j + 1) * SLOTS)
        keep(s, 2 * i + j, G_EPS, tile_sum(x1[:, lanes] * s["wout"][...]))
    high, low = split(x1)
    s["x1f"][i] = x1
    s["x1"][i, 0:CH, :] = high
    s["x1"][i, CH : 2 * CH, :] = low
    yield
    s["mix"][i] = dot(s["a3"][...], jnp.concatenate([high, low, high], axis=0))


def sincospi(part):
    t = part * math.pi
    q = t * t
    sine = 1.0 / 6227020800.0
    for c in (-1.0 / 39916800, 1.0 / 362880, -1.0 / 5040, 1.0 / 120, -1.0 / 6):
        sine = sine * q + c
    sine = t + t * (q * sine)
    cosine = -1.0 / 87178291200.0
    for c in (1.0 / 479001600, -1.0 / 3628800, 1.0 / 40320, -1.0 / 720, 1.0 / 24, -0.5, 1.0):
        cosine = cosine * q + c
    return sine, cosine


def accumulate(source, level_rows, s, target):
    for chan in range(0, CH, BLOCK):
        total = [None] * 9
        for i in range(PAIRS):
            for j in range(2):
                lanes = slice(j * SLOTS, (j + 1) * SLOTS)
                starts = [l * level_rows + chan for l in range(3 if level_rows else 1)]
                parts = [source[i, a : a + BLOCK, lanes] for a in starts]
                for m in range(9):
                    part = parts[LEVEL[m] if level_rows else 0]
                    if m:
                        part = part * tall(row(s, 2 * i + j, HARM + m - 1), BLOCK // 8)
                    total[m] = part if total[m] is None else total[m] + part
        for m in range(9):
            target[chan : chan + BLOCK, m * SLOTS : (m + 1) * SLOTS] = total[m]


def mix_levels(weights, source, target):
    for level, (low, high) in enumerate(((0, 1), (1, 4), (4, 9))):
        lanes = slice(low * SLOTS, high * SLOTS)
        mixed = dot(weights[level], stack3(source[:, lanes]))
        for m in range(low, high):
            target[m] = mixed[:, (m - low) * SLOTS : (m - low + 1) * SLOTS]


def project(ys, fields):
    out = [fields[0], None, None]
    for m in range(1, 9):
        term = ys[m] * fields[m]
        level = LEVEL[m]
        out[level] = term if out[level] is None else out[level] + term
    return out


def harmonics_of(s, k):
    return [None] + [row(s, k, HARM + m - 1) for m in range(1, 9)]


def tensors(i, s):
    for j in range(2):
        lanes = slice(j * SLOTS, (j + 1) * SLOTS)
        ys = harmonics_of(s, 2 * i + j)
        for c in range(0, CH, 16):
            tiles = [[], [], []]
            for chan in (c, c + 8):
                fields = [s["vec"][m, chan : chan + 8, :] for m in range(9)]
                for level, tile in enumerate(project(ys, fields)):
                    tiles[level].append(tile)
            for level in range(3):
                proj = jnp.concatenate(tiles[level], axis=0)
                at = level * CH + c
                s["proj"][i, at : at + 16, lanes] = proj
                high, low = split(s["mix"][i, at : at + 16, lanes] * proj)
                s["scal"][i, at : at + 16, lanes] = high
                s["scal"][i, 3 * CH + at : 3 * CH + at + 16, lanes] = low


def three_body(i, s):
    if FOLD[0]:
        tensors(i, s)
        yield
    high = s["scal"][i, 0 : 3 * CH, :]
    low = s["scal"][i, 3 * CH : 6 * CH, :]
    x1h = s["x1"][i, 0:CH, :]
    x1l = s["x1"][i, CH : 2 * CH, :]
    z = tall_dot(
        s["a4"], jnp.concatenate([x1h, high], axis=0), jnp.concatenate([x1l, low], axis=0)
    )
    act, dact = silu_pair(z)
    wout = s["wout"][...]
    for j in range(2):
        k = 2 * i + j
        lanes = slice(j * SLOTS, (j + 1) * SLOTS)
        rows = pl.ds((k * PART + G_EPS) * 8, 8)
        s["part"][rows, :] = s["part"][rows, :] + tile_sum(act[:, lanes] * wout)
    gout = jnp.concatenate([wout * tall(row(s, 2 * i + j, ENV), 8) for j in range(2)], axis=1)
    gz = stack3(gout * dact)
    yield
    gj = dot(s["a5"][...], gz)
    s["gx1"][i] = gout + gj[:CH]
    gs = gj[CH:]
    s["q"][i] = gs * s["mix"][i]
    high, low = split(gs * s["proj"][i])
    yield
    s["gx1"][i] = s["gx1"][i] + tall_dot(s["a6"], high, low)


def flows(i, s):
    for j in range(2):
        k = 2 * i + j
        lanes = slice(j * SLOTS, (j + 1) * SLOTS)
        ys = harmonics_of(s, k)
        turns = [None] * 9
        for c in range(0, CH, 8):
            chan = slice(c, c + 8)
            qs = [s["q"][i, l * CH + c : l * CH + c + 8, lanes] for l in range(3)]
            x1 = s["x1f"][i, chan, lanes]
            flow = s["gx1"][i, chan, lanes] + s["gvec"][0, chan, :]
            for m in range(1, 9):
                gfield = s["gvec"][m, chan, :]
                flow = flow + ys[m] * gfield
                both = qs[LEVEL[m]] * s["vec"][m, chan, :] + x1 * gfield
                turns[m] = both if c == 0 else turns[m] + both
            s["gx1"][i, chan, lanes] = flow
        for m in range(1, 9):
            keep(s, k, G_HARM + m - 1, turns[m])


def backward(i, s):
    if FOLD[1]:
        flows(i, s)
        yield
    gx1 = s["gx1"][i]
    genv = tile_sum(gx1 * s["s2"][i])
    gh = stack3(gx1 * s["d2"][i])
    yield
    gh = stack3(dot(s["a7"][...], gh) * s["dh"][i])
    yield
    gb = dot(s["a8"][...], gh)
    for j in range(2):
        k = 2 * i + j
        lanes = slice(j * SLOTS, (j + 1) * SLOTS)
        keep(s, k, G_ENV, genv[:, lanes])
        keep(s, k, G_RAD, gb[:, lanes] * s["dbas"][k])


def edge_forces(tile, nbr, total, s):
    rows = pl.ds(tile * 8, 8)
    valid = nbr[rows, :] >= 0
    ux, uy, uz, inv, denv, env = (s["dense"][r, rows, :] for r in range(6))

    def whole(r):
        return total_of(
            [
                s["part"][pl.ds((tile * 8 * PART + r) * 8 + lane, 8, stride=8 * PART), :]
                for lane in range(8)
            ]
        )

    y = [None] + [whole(G_HARM + m - 1) for m in range(1, 9)]
    eps = whole(G_EPS)
    gx = ROOT3 * y[1] + ROOT15 * (uy * y[4] + uz * y[7] + ux * y[8])
    gy = ROOT3 * y[2] + ROOT15 * (ux * y[4] + uz * y[5] - uy * y[8])
    gz = ROOT3 * y[3] + ROOT15 * (uy * y[5] + ux * y[7]) + (3.0 * ROOT5) * (uz * y[6])
    along = ux * gx + uy * gy + uz * gz
    radial = whole(G_RAD) + (whole(G_ENV) + eps) * denv - along * inv
    for c, (unit, g) in enumerate(((ux, gx), (uy, gy), (uz, gz))):
        value = jnp.where(valid, radial * unit + g * inv, 0.0)
        high = value.astype(BF16).astype(F32)
        s["gr"][pl.ds(tile * 64 + c, 8, stride=8), :] = high
        s["gr"][pl.ds(tile * 64 + 3 + c, 8, stride=8), :] = value - high
        total[c] = total[c] + value
    total[3] = total[3] + jnp.where(valid, eps * env, 0.0)


def prepare_scatter(i, nbr, s):
    for j in range(2):
        k = 2 * i + j
        safe = jnp.maximum(nbr[pl.ds(k, 1), :], 0)
        here = lax.broadcasted_iota(jnp.int32, (32, SLOTS), 0) == (safe >> 7)
        s["codes"][k] = jnp.where(here, 1.0, 0.0)
        slot = lax.broadcasted_iota(jnp.int32, (SLOTS, SLOTS), 0) == (safe & 127)
        lanes = pl.ds(pl.multiple_of(k * SLOTS, SLOTS), SLOTS)
        s["hot"][:, lanes] = jnp.where(slot, 1.0, 0.0).astype(BF16)


def scatter(tile, s):
    entries = range(tile * 8, min(tile * 8 + 8, LIST))
    columns = []
    for k in entries:
        codes = s["codes"][k]
        rows = [s["gr"][k * 8 + c : k * 8 + c + 1, :] for c in range(6)]
        columns.append(jnp.concatenate([codes * r for r in rows], axis=0).astype(BF16))
    return lax.dot_general(
        jnp.concatenate(columns, axis=1),
        s["hot"][:, entries[0] * SLOTS : (entries[-1] + 1) * SLOTS],
        (((1,), (1,)), ((), ())),
        preferred_element_type=F32,
    )


def total_of(terms):
    while len(terms) > 1:
        terms = [sum(terms[i : i + 2][1:], terms[i]) for i in range(0, len(terms), 2)]
    return terms[0]


def loop(body):
    lax.fori_loop(0, PAIRS, lambda i, carry: (body(i), carry)[1], 0)


def staggered(body, group, then=None):
    ended = 0
    waiting = [range(a, min(a + group, PAIRS)) for a in range(0, PAIRS, group)]
    live = []
    while waiting or live:
        if waiting:
            live.append([body(i) for i in waiting.pop(0)])
        live = [[stage for stage in one if next(stage, True) is None] for one in live]
        if not live[0]:
            live = live[1:]
            if then:
                then(ended)
            ended += 1


GROUPS = (5, 5)
FOLD = (True, True)


def compute(table, nbr, pos, spec, s):
    geometry(table, nbr, pos, s)
    order = lax.broadcasted_iota(jnp.int32, (8, SLOTS), 0)
    center_hot = jnp.where(spec == order, 1.0, 0.0)
    staggered(lambda i: two_body(i, s, center_hot), GROUPS[0])
    accumulate(s["x1f"], 0, s, s["sums"])
    mix_levels(s["ae"], s["sums"], s["vec"])
    if not FOLD[0]:
        loop(lambda i: tensors(i, s))
    staggered(lambda i: three_body(i, s), GROUPS[1])
    accumulate(s["q"], CH, s, s["sums"])
    mix_levels(s["ag"], s["sums"], s["gvec"])
    if not FOLD[1]:
        loop(lambda i: flows(i, s))
    total = [jnp.zeros((8, SLOTS), F32) for _ in range(4)]
    spread = []

    def finish(tile):
        edge_forces(tile, nbr, total, s)
        spread.append(scatter(tile, s))

    staggered(lambda i: backward(i, s), 4, finish)
    center = [jnp.sum(part, axis=0, keepdims=True) for part in total]
    spread = total_of(spread)
    return center[3], center[:3], spread[:96] + spread[96:]


WEIGHTS = ("emb_center", "emb_neigh", "w_radial", "w_two", "w_pair", "w_latent", "w_out")
WIDE = 2 * SLOTS
SCRATCH = {
    "a1": ((CH, 64), BF16),
    "a2": ((CH, 192), BF16),
    "a3": ((3 * CH, 192), BF16),
    "a4": ((2 * CH, 256), BF16),
    "a5": ((4 * CH, 192), BF16),
    "a6": ((2 * CH, 192), BF16),
    "ae": ((3, CH, 192), BF16),
    "ag": ((3, CH, 192), BF16),
    "sums": ((CH, 9 * SLOTS), F32),
    "x1f": ((PAIRS, CH, WIDE), F32),
    "proj": ((PAIRS, 3 * CH, WIDE), F32),
    "a7": ((CH, 192), BF16),
    "a8": ((8, 192), BF16),
    "wout": ((CH, SLOTS), F32),
    "geo": ((32 * GEO, SLOTS), F32),
    "dense": ((6, 32, SLOTS), F32),
    "dbas": ((LIST, 8, SLOTS), F32),
    "dh": ((PAIRS, CH, WIDE), F32),
    "s2": ((PAIRS, CH, WIDE), F32),
    "d2": ((PAIRS, CH, WIDE), F32),
    "x1": ((PAIRS, 2 * CH, WIDE), BF16),
    "mix": ((PAIRS, 3 * CH, WIDE), F32),
    "vec": ((9, CH, SLOTS), F32),
    "gvec": ((9, CH, SLOTS), F32),
    "gx1": ((PAIRS, CH, WIDE), F32),
    "scal": ((PAIRS, 6 * CH, WIDE), BF16),
    "q": ((PAIRS, 3 * CH, WIDE), F32),
    "part": ((32 * PART * 8, SLOTS), F32),
    "gr": ((32 * 8, SLOTS), F32),
    "nbr": ((32, SLOTS), jnp.int32),
    "codes": ((LIST, 32, SLOTS), F32),
    "hot": ((SLOTS, LIST * SLOTS), BF16),
}


def neighbour(shift, sizes):
    return tuple(
        lax.rem(lax.axis_index(axis) + (d + size), size)
        for (axis, size), d in zip(sizes, shift)
    )


FAR_FIRST = sorted(OTHERS, key=lambda n: -sum(w * abs(d) for w, d in zip((2, 1, 2), SHIFTS[n])))


def kernel(sizes, *refs):
    inputs = refs[:10]
    energy_out, force_out = refs[10:12]
    scratch = dict(zip(SCRATCH, refs[12 : 12 + len(SCRATCH)]))
    refs = refs[12 + len(SCRATCH) :]
    copied, weights = refs[:7], dict(zip(WEIGHTS, refs[:7]))
    packed, table, outbox, inbox, spec_ref, send, recv, send_back, recv_back, sems = refs[7:]
    nbr = scratch["nbr"]

    def remote(src, dst, pair, n):
        return pltpu.make_async_remote_copy(
            src_ref=src,
            dst_ref=dst,
            send_sem=pair[0],
            recv_sem=pair[1],
            device_id=neighbour(SHIFTS[n], sizes),
            device_id_type=MESH,
        )

    own = [
        pltpu.make_async_copy(inputs[1].at[0, 0], spec_ref, sems.at[0]),
        pltpu.make_async_copy(inputs[0].at[:, 0, 0, 0, :], packed.at[0:3], sems.at[1]),
        pltpu.make_async_copy(inputs[2].at[0, 0, :, 0, :], nbr.at[0:LIST, :], sems.at[2]),
    ]
    own += [
        pltpu.make_async_copy(src, dst, sems.at[3 + i])
        for i, (src, dst) in enumerate(zip(inputs[3:], copied))
    ]
    own[0].start()
    own[1].start()
    barrier = pltpu.get_barrier_semaphore()
    for n in FAR_FIRST:
        pl.semaphore_signal(
            barrier, inc=1, device_id=neighbour(SHIFTS[n], sizes), device_id_type=MESH
        )
    for copy in own[2:]:
        copy.start()
    nbr[LIST:, :] = jnp.full((32 - LIST, SLOTS), -1, jnp.int32)
    outbox[:, 3, :] = jnp.zeros((32, SLOTS), F32)
    own[0].wait()
    spec = spec_ref[...]
    packed[3:4, :] = spec.astype(F32)
    own[1].wait()
    pl.semaphore_wait(barrier, 26)

    for n in FAR_FIRST:
        remote(packed, table.at[PLACE[26 - n]], (send, recv), n).start()
    table[26] = packed[...]
    pos = packed[0:3, :]
    for copy in own[2:]:
        copy.wait()
    prepare_weights(weights, scratch)
    loop(lambda i: prepare_scatter(i, nbr, scratch))
    everyone = table.at[0:26]
    remote(everyone, everyone, (send, recv), 0).wait()

    energy, center, spread = compute(table, nbr, pos, spec, scratch)
    for c in range(3):
        outbox[:, c, :] = spread[c * 32 : (c + 1) * 32]
    for n in FAR_FIRST:
        remote(outbox.at[n], inbox.at[PLACE[26 - n]], (send_back, recv_back), n).start()
    energy_out[0, 0] = energy
    force = jnp.concatenate(center, axis=0) - outbox[13, 0:3, :]
    everyone = inbox.at[0:26]
    remote(everyone, everyone, (send_back, recv_back), 0).wait()
    force_out[:, 0, 0, 0, :] = force - total_of([inbox[i, 0:3, :] for i in range(26)])


def solution(mesh):
    sizes = tuple((axis, mesh.shape[axis]) for axis in ("gx", "gy", "gz"))

    def local(positions, species, neighbours, emb_c, emb_n, w_rad, w_two, w_pair, w_lat, w_out):
        vmem = pl.BlockSpec(memory_space=pltpu.VMEM)
        dma = pltpu.SemaphoreType.DMA
        weights = (emb_c, emb_n, w_rad, w_two, w_pair, w_lat.T, w_out.reshape(1, CH))
        return pl.pallas_call(
            functools.partial(kernel, sizes),
            out_shape=(
                pltpu.VMEM(species.shape, F32),
                pltpu.VMEM(positions.shape, F32),
            ),
            in_specs=[pl.BlockSpec(memory_space=pl.ANY)] * 10,
            out_specs=(vmem, vmem),
            scratch_shapes=[pltpu.VMEM(*spec) for spec in SCRATCH.values()]
            + [pltpu.VMEM(w.shape, F32) for w in weights]
            + [
                pltpu.VMEM((4, SLOTS), F32),
                pltpu.VMEM((27, 4, SLOTS), F32),
                pltpu.VMEM((32, 4, SLOTS), F32),
                pltpu.VMEM((26, 4, SLOTS), F32),
                pltpu.VMEM((1, SLOTS), jnp.int32),
            ]
            + [dma] * 4
            + [dma((10,))],
            compiler_params=pltpu.CompilerParams(
                collective_id=0, has_side_effects=True, vmem_limit_bytes=60 << 20
            ),
        )(positions, species, jnp.swapaxes(neighbours, 2, 3), *weights)

    placed = (
        P(None, "gx", "gy", "gz", None),
        P("gx", "gy", "gz", None),
        P("gx", "gy", "gz", None, None),
    ) + (P(),) * 7
    return jax.shard_map(
        local,
        mesh=mesh,
        in_specs=placed,
        out_specs=(P("gx", "gy", "gz", None), P(None, "gx", "gy", "gz", None)),
        check_vma=False,
    )
```

```python
import functools
import math

import jax
import jax.numpy as jnp
from jax import lax
from jax.experimental import pallas as pl
from jax.experimental.pallas import tpu as pltpu
from jax.sharding import PartitionSpec as P

MESH = pl.DeviceIdType.MESH
F32 = jnp.float32
BF16 = jnp.bfloat16
RADIUS = 5.0
EDGES = (8.6, 8.6, 17.2)
SCALE = 0.125
CH = 64
SLOTS = 128
LIST = 26
PAIRS = LIST // 2
NSPEC = 5
LEVEL = (0, 1, 1, 1, 2, 2, 2, 2, 2)
SHIFTS = tuple((x, y, z) for x in (-1, 0, 1) for y in (-1, 0, 1) for z in (-1, 0, 1))
OTHERS = [n for n in range(27) if n != 13]
FAR = [n for n in OTHERS if all(SHIFTS[n])]
NEAR = [n for n in OTHERS if n not in FAR]
PLACE = {n: place for place, n in enumerate(NEAR + FAR)} | {13: 26}
XS, INVD, ENV, KIND, HARM = 0, 1, 2, 3, 4
G_RAD, G_ENV, G_EPS, G_HARM = 0, 1, 2, 3
GEO, PART = 16, 11
BLOCK = 16
ROOT3, ROOT5, ROOT15 = math.sqrt(3.0), math.sqrt(5.0), math.sqrt(15.0)


def split(x):
    high = x.astype(BF16)
    low = (x - high.astype(F32)).astype(BF16)
    return high, low


def stack3(x):
    high, low = split(x)
    return jnp.concatenate([high, low, high], axis=0)


def dot(lhs, rhs):
    return jnp.dot(lhs, rhs, preferred_element_type=F32)


def tall_dot(weights, high, low):
    both = dot(weights[...], high)
    rows = both.shape[0] // 2
    return both[:rows] + both[rows:] + dot(weights[0:rows, :], low)


def silu_pair(half):
    turn = jnp.tanh(half)
    act = half + half * turn
    return act, act - act * turn + turn + 1.0


def transpose_stack(w):
    high = w.astype(BF16).astype(F32)
    return jnp.concatenate([high, high, w - high], axis=0).T.astype(BF16)


def prepare_weights(w, s):
    zero = lambda rows: jnp.zeros((rows, CH), F32)
    parts = []
    radial = w["w_radial"][...]
    rh = radial.astype(BF16).astype(F32)
    parts += [rh, rh, radial - rh]
    for name in ("emb_neigh", "emb_center"):
        emb = w[name][...]
        eh = emb.astype(BF16).astype(F32)
        parts += [jnp.concatenate([eh, zero(8 - NSPEC)], axis=0)]
        parts += [jnp.concatenate([emb - eh, zero(8 - NSPEC)], axis=0)]
    parts += [zero(8)]
    s["a1"][...] = (0.5 * jnp.concatenate(parts, axis=0)).T.astype(BF16)
    two = w["w_two"][...]
    s["a2"][...] = transpose_stack(0.5 * two)
    s["a7"][...] = transpose_stack(0.5 * two.T)
    s["a8"][...] = transpose_stack(0.5 * radial.T)
    pair = w["w_pair"][...]
    s["a3"][...] = transpose_stack(pair[:, 3 * CH :])
    turned = pair.T
    s["a6"][...] = jnp.concatenate(split(pair[:, 3 * CH :]), axis=0)
    for level in range(3):
        s["ae"][level] = transpose_stack(SCALE * pair[:, level * CH : (level + 1) * CH])
        s["ag"][level] = transpose_stack(SCALE * turned[level * CH : (level + 1) * CH])
    latent = w["w_latent"][...]
    s["a4"][...] = jnp.concatenate(split(0.5 * latent), axis=0)
    s["a5"][...] = transpose_stack(0.5 * latent)
    s["wout"][...] = jnp.broadcast_to(w["w_out"][...].T, (CH, SLOTS))


def gather(table, nbr, codes, got):
    for tile in range(4):
        safe = jnp.maximum(nbr[pl.ds(tile * 8, 8), :], 0)
        slot = safe & 127
        for n in codes:
            here = (safe >> 7) == n
            for c in range(4):
                source = jnp.broadcast_to(table[PLACE[n], c : c + 1, :], (8, SLOTS))
                value = jnp.take_along_axis(source, slot, axis=1, mode="promise_in_bounds")
                if c < 3 and SHIFTS[n][c]:
                    value = value + SHIFTS[n][c] * EDGES[c]
                got[tile][c] = jnp.where(here, value, got[tile][c])


def geometry(table, nbr, pos, s, arrive):
    found = [[jnp.zeros((8, SLOTS), F32) for _ in range(4)] for _ in range(4)]
    gather(table, nbr, [13] + NEAR, found)
    arrive()
    gather(table, nbr, FAR, found)
    for tile, got in enumerate(found):
        rows = pl.ds(tile * 8, 8)
        valid = nbr[rows, :] >= 0
        delta = [jnp.where(valid, got[c] - pos[c : c + 1, :], 1.0) for c in range(3)]
        square = delta[0] * delta[0] + delta[1] * delta[1] + delta[2] * delta[2]
        dist = jnp.sqrt(square)
        inv = 1.0 / dist
        ux, uy, uz = (d * inv for d in delta)
        scaled = dist * (1.0 / RADIUS)
        inside = jnp.logical_and(valid, scaled < 1.0)
        sq = scaled * scaled
        p5 = sq * sq * scaled
        p6 = p5 * scaled
        env = 1.0 + p6 * (-28.0 + scaled * (48.0 - 21.0 * scaled))
        denv = (1.0 / RADIUS) * p5 * (-168.0 + scaled * (336.0 - 168.0 * scaled))
        env = jnp.where(inside, env, 0.0)
        denv = jnp.where(inside, denv, 0.0)
        values = [jnp.minimum(scaled, 1.0), inv, env, got[3]]
        values += [ROOT3 * ux, ROOT3 * uy, ROOT3 * uz, ROOT15 * ux * uy, ROOT15 * uy * uz]
        values += [0.5 * ROOT5 * (3.0 * uz * uz - 1.0), ROOT15 * ux * uz]
        values += [0.5 * ROOT15 * (ux * ux - uy * uy)]
        for r, v in enumerate(values):
            s["geo"][pl.ds(tile * 8 * GEO + r, 8, stride=GEO), :] = v
        for r, v in enumerate((ux, uy, uz, inv, denv, env)):
            s["dense"][r, rows, :] = v


def row(s, k, r):
    return jnp.broadcast_to(s["geo"][pl.ds(k * GEO + r, 1), :], (8, SLOTS))


def tile_sum(x):
    return jnp.sum(x.reshape(x.shape[0] // 8, 8, x.shape[1]), axis=0)


def tall(tile, count):
    return jnp.concatenate([tile] * count, axis=0)


def keep(s, k, r, tile):
    start = (k * PART + r) * 8
    s["part"][pl.ds(start if isinstance(start, int) else pl.multiple_of(start, 8), 8), :] = tile


def two_body(i, s, center_hot):
    order = lax.broadcasted_iota(jnp.int32, (8, SLOTS), 0).astype(F32)
    columns = []
    for j in range(2):
        k = 2 * i + j
        turns = (order + 1.0) * row(s, k, XS)
        inv = row(s, k, INVD)
        whole = jnp.floor(turns + 0.5)
        part = turns - whole
        odd = whole - 2.0 * jnp.floor(0.5 * whole)
        sign = (1.0 - 2.0 * odd) * (math.sqrt(2.0 / RADIUS) * inv)
        sine, cosine = sincospi(part)
        basis = sign * sine
        s["dbas"][k] = (sign * cosine) * ((order + 1.0) * (math.pi / RADIUS)) - basis * inv
        hot = jnp.where(row(s, k, KIND) == order, 1.0, 0.0)
        high = basis.astype(BF16).astype(F32)
        zero = jnp.zeros((8, SLOTS), F32)
        columns.append(
            jnp.concatenate(
                [high, basis - high, high, hot, hot, center_hot, center_hot, zero], axis=0
            ).astype(BF16)
        )
    columns = jnp.concatenate(columns, axis=1)
    yield
    act, dact = silu_pair(dot(s["a1"][...], columns))
    s["dh"][i] = dact
    act = stack3(act)
    yield
    act2, dact2 = silu_pair(dot(s["a2"][...], act))
    env = jnp.concatenate([tall(row(s, 2 * i + j, ENV), 8) for j in range(2)], axis=1)
    s["s2"][i] = act2
    s["d2"][i] = dact2 * env
    x1 = act2 * env
    for j in range(2):
        lanes = slice(j * SLOTS, (j + 1) * SLOTS)
        keep(s, 2 * i + j, G_EPS, tile_sum(x1[:, lanes] * s["wout"][...]))
    high, low = split(x1)
    s["x1f"][i] = x1
    s["x1"][i, 0:CH, :] = high
    s["x1"][i, CH : 2 * CH, :] = low
    yield
    s["mix"][i] = dot(s["a3"][...], jnp.concatenate([high, low, high], axis=0))


def sincospi(part):
    t = part * math.pi
    q = t * t
    sine = 1.0 / 6227020800.0
    for c in (-1.0 / 39916800, 1.0 / 362880, -1.0 / 5040, 1.0 / 120, -1.0 / 6):
        sine = sine * q + c
    sine = t + t * (q * sine)
    cosine = -1.0 / 87178291200.0
    for c in (1.0 / 479001600, -1.0 / 3628800, 1.0 / 40320, -1.0 / 720, 1.0 / 24, -0.5, 1.0):
        cosine = cosine * q + c
    return sine, cosine


def accumulate(source, level_rows, s, target):
    for chan in range(0, CH, BLOCK):
        total = [None] * 9
        for i in range(PAIRS):
            for j in range(2):
                lanes = slice(j * SLOTS, (j + 1) * SLOTS)
                starts = [l * level_rows + chan for l in range(3 if level_rows else 1)]
                parts = [source[i, a : a + BLOCK, lanes] for a in starts]
                for m in range(9):
                    part = parts[LEVEL[m] if level_rows else 0]
                    if m:
                        part = part * tall(row(s, 2 * i + j, HARM + m - 1), BLOCK // 8)
                    total[m] = part if total[m] is None else total[m] + part
        for m in range(9):
            target[chan : chan + BLOCK, m * SLOTS : (m + 1) * SLOTS] = total[m]


def mix_levels(weights, source, target):
    for level, (low, high) in enumerate(((0, 1), (1, 4), (4, 9))):
        lanes = slice(low * SLOTS, high * SLOTS)
        mixed = dot(weights[level], stack3(source[:, lanes]))
        for m in range(low, high):
            target[m] = mixed[:, (m - low) * SLOTS : (m - low + 1) * SLOTS]


def project(ys, fields):
    out = [fields[0], None, None]
    for m in range(1, 9):
        term = ys[m] * fields[m]
        level = LEVEL[m]
        out[level] = term if out[level] is None else out[level] + term
    return out


def harmonics_of(s, k):
    return [None] + [row(s, k, HARM + m - 1) for m in range(1, 9)]


def tensors(i, s):
    for j in range(2):
        lanes = slice(j * SLOTS, (j + 1) * SLOTS)
        ys = harmonics_of(s, 2 * i + j)
        for c in range(0, CH, 16):
            tiles = [[], [], []]
            for chan in (c, c + 8):
                fields = [s["vec"][m, chan : chan + 8, :] for m in range(9)]
                for level, tile in enumerate(project(ys, fields)):
                    tiles[level].append(tile)
            for level in range(3):
                proj = jnp.concatenate(tiles[level], axis=0)
                at = level * CH + c
                s["proj"][i, at : at + 16, lanes] = proj
                high, low = split(s["mix"][i, at : at + 16, lanes] * proj)
                s["scal"][i, at : at + 16, lanes] = high
                s["scal"][i, 3 * CH + at : 3 * CH + at + 16, lanes] = low


def three_body(i, s):
    if FOLD[0]:
        tensors(i, s)
        yield
    high = s["scal"][i, 0 : 3 * CH, :]
    low = s["scal"][i, 3 * CH : 6 * CH, :]
    x1h = s["x1"][i, 0:CH, :]
    x1l = s["x1"][i, CH : 2 * CH, :]
    z = tall_dot(
        s["a4"], jnp.concatenate([x1h, high], axis=0), jnp.concatenate([x1l, low], axis=0)
    )
    act, dact = silu_pair(z)
    wout = s["wout"][...]
    for j in range(2):
        k = 2 * i + j
        lanes = slice(j * SLOTS, (j + 1) * SLOTS)
        rows = pl.ds((k * PART + G_EPS) * 8, 8)
        s["part"][rows, :] = s["part"][rows, :] + tile_sum(act[:, lanes] * wout)
    gout = jnp.concatenate([wout * tall(row(s, 2 * i + j, ENV), 8) for j in range(2)], axis=1)
    gz = stack3(gout * dact)
    yield
    gj = dot(s["a5"][...], gz)
    s["gx1"][i] = gout + gj[:CH]
    gs = gj[CH:]
    s["q"][i] = gs * s["mix"][i]
    high, low = split(gs * s["proj"][i])
    yield
    s["gx1"][i] = s["gx1"][i] + tall_dot(s["a6"], high, low)


def flows(i, s):
    for j in range(2):
        k = 2 * i + j
        lanes = slice(j * SLOTS, (j + 1) * SLOTS)
        ys = harmonics_of(s, k)
        turns = [None] * 9
        for c in range(0, CH, 8):
            chan = slice(c, c + 8)
            qs = [s["q"][i, l * CH + c : l * CH + c + 8, lanes] for l in range(3)]
            x1 = s["x1f"][i, chan, lanes]
            flow = s["gx1"][i, chan, lanes] + s["gvec"][0, chan, :]
            for m in range(1, 9):
                gfield = s["gvec"][m, chan, :]
                flow = flow + ys[m] * gfield
                both = qs[LEVEL[m]] * s["vec"][m, chan, :] + x1 * gfield
                turns[m] = both if c == 0 else turns[m] + both
            s["gx1"][i, chan, lanes] = flow
        for m in range(1, 9):
            keep(s, k, G_HARM + m - 1, turns[m])


def backward(i, s):
    if FOLD[1]:
        flows(i, s)
        yield
    gx1 = s["gx1"][i]
    genv = tile_sum(gx1 * s["s2"][i])
    gh = stack3(gx1 * s["d2"][i])
    yield
    gh = stack3(dot(s["a7"][...], gh) * s["dh"][i])
    yield
    gb = dot(s["a8"][...], gh)
    for j in range(2):
        k = 2 * i + j
        lanes = slice(j * SLOTS, (j + 1) * SLOTS)
        keep(s, k, G_ENV, genv[:, lanes])
        keep(s, k, G_RAD, gb[:, lanes] * s["dbas"][k])


def edge_forces(tile, nbr, total, s):
    rows = pl.ds(tile * 8, 8)
    valid = nbr[rows, :] >= 0
    ux, uy, uz, inv, denv, env = (s["dense"][r, rows, :] for r in range(6))

    def whole(r):
        return total_of(
            [
                s["part"][pl.ds((tile * 8 * PART + r) * 8 + lane, 8, stride=8 * PART), :]
                for lane in range(8)
            ]
        )

    y = [None] + [whole(G_HARM + m - 1) for m in range(1, 9)]
    eps = whole(G_EPS)
    gx = ROOT3 * y[1] + ROOT15 * (uy * y[4] + uz * y[7] + ux * y[8])
    gy = ROOT3 * y[2] + ROOT15 * (ux * y[4] + uz * y[5] - uy * y[8])
    gz = ROOT3 * y[3] + ROOT15 * (uy * y[5] + ux * y[7]) + (3.0 * ROOT5) * (uz * y[6])
    along = ux * gx + uy * gy + uz * gz
    radial = whole(G_RAD) + (whole(G_ENV) + eps) * denv - along * inv
    for c, (unit, g) in enumerate(((ux, gx), (uy, gy), (uz, gz))):
        value = jnp.where(valid, radial * unit + g * inv, 0.0)
        high = value.astype(BF16).astype(F32)
        s["gr"][pl.ds(tile * 64 + c, 8, stride=8), :] = high
        s["gr"][pl.ds(tile * 64 + 3 + c, 8, stride=8), :] = value - high
        total[c] = total[c] + value
    total[3] = total[3] + jnp.where(valid, eps * env, 0.0)


def prepare_scatter(i, nbr, s):
    for j in range(2):
        k = 2 * i + j
        safe = jnp.maximum(nbr[pl.ds(k, 1), :], 0)
        here = lax.broadcasted_iota(jnp.int32, (32, SLOTS), 0) == (safe >> 7)
        s["codes"][k] = jnp.where(here, 1.0, 0.0)
        slot = lax.broadcasted_iota(jnp.int32, (SLOTS, SLOTS), 0) == (safe & 127)
        lanes = pl.ds(pl.multiple_of(k * SLOTS, SLOTS), SLOTS)
        s["hot"][:, lanes] = jnp.where(slot, 1.0, 0.0).astype(BF16)


def scatter(tile, s):
    entries = range(tile * 8, min(tile * 8 + 8, LIST))
    columns = []
    for k in entries:
        codes = s["codes"][k]
        rows = [s["gr"][k * 8 + c : k * 8 + c + 1, :] for c in range(6)]
        columns.append(jnp.concatenate([codes * r for r in rows], axis=0).astype(BF16))
    return lax.dot_general(
        jnp.concatenate(columns, axis=1),
        s["hot"][:, entries[0] * SLOTS : (entries[-1] + 1) * SLOTS],
        (((1,), (1,)), ((), ())),
        preferred_element_type=F32,
    )


def total_of(terms):
    while len(terms) > 1:
        terms = [sum(terms[i : i + 2][1:], terms[i]) for i in range(0, len(terms), 2)]
    return terms[0]


def loop(body):
    lax.fori_loop(0, PAIRS, lambda i, carry: (body(i), carry)[1], 0)


def staggered(body, group, then=None):
    ended = 0
    waiting = [range(a, min(a + group, PAIRS)) for a in range(0, PAIRS, group)]
    live = []
    while waiting or live:
        if waiting:
            live.append([body(i) for i in waiting.pop(0)])
        live = [[stage for stage in one if next(stage, True) is None] for one in live]
        if not live[0]:
            live = live[1:]
            if then:
                then(ended)
            ended += 1


GROUPS = (5, 5)
FOLD = (True, True)


def compute(table, nbr, pos, spec, s, arrive=lambda: None):
    geometry(table, nbr, pos, s, arrive)
    order = lax.broadcasted_iota(jnp.int32, (8, SLOTS), 0)
    center_hot = jnp.where(spec == order, 1.0, 0.0)
    staggered(lambda i: two_body(i, s, center_hot), GROUPS[0])
    accumulate(s["x1f"], 0, s, s["sums"])
    mix_levels(s["ae"], s["sums"], s["vec"])
    if not FOLD[0]:
        loop(lambda i: tensors(i, s))
    staggered(lambda i: three_body(i, s), GROUPS[1])
    accumulate(s["q"], CH, s, s["sums"])
    mix_levels(s["ag"], s["sums"], s["gvec"])
    if not FOLD[1]:
        loop(lambda i: flows(i, s))
    total = [jnp.zeros((8, SLOTS), F32) for _ in range(4)]
    spread = []

    def finish(tile):
        edge_forces(tile, nbr, total, s)
        spread.append(scatter(tile, s))

    staggered(lambda i: backward(i, s), 4, finish)
    center = [jnp.sum(part, axis=0, keepdims=True) for part in total]
    spread = total_of(spread)
    return center[3], center[:3], spread[:96] + spread[96:]


WEIGHTS = ("emb_center", "emb_neigh", "w_radial", "w_two", "w_pair", "w_latent", "w_out")
WIDE = 2 * SLOTS
SCRATCH = {
    "a1": ((CH, 64), BF16),
    "a2": ((CH, 192), BF16),
    "a3": ((3 * CH, 192), BF16),
    "a4": ((2 * CH, 256), BF16),
    "a5": ((4 * CH, 192), BF16),
    "a6": ((2 * CH, 192), BF16),
    "ae": ((3, CH, 192), BF16),
    "ag": ((3, CH, 192), BF16),
    "sums": ((CH, 9 * SLOTS), F32),
    "x1f": ((PAIRS, CH, WIDE), F32),
    "proj": ((PAIRS, 3 * CH, WIDE), F32),
    "a7": ((CH, 192), BF16),
    "a8": ((8, 192), BF16),
    "wout": ((CH, SLOTS), F32),
    "geo": ((32 * GEO, SLOTS), F32),
    "dense": ((6, 32, SLOTS), F32),
    "dbas": ((LIST, 8, SLOTS), F32),
    "dh": ((PAIRS, CH, WIDE), F32),
    "s2": ((PAIRS, CH, WIDE), F32),
    "d2": ((PAIRS, CH, WIDE), F32),
    "x1": ((PAIRS, 2 * CH, WIDE), BF16),
    "mix": ((PAIRS, 3 * CH, WIDE), F32),
    "vec": ((9, CH, SLOTS), F32),
    "gvec": ((9, CH, SLOTS), F32),
    "gx1": ((PAIRS, CH, WIDE), F32),
    "scal": ((PAIRS, 6 * CH, WIDE), BF16),
    "q": ((PAIRS, 3 * CH, WIDE), F32),
    "part": ((32 * PART * 8, SLOTS), F32),
    "gr": ((32 * 8, SLOTS), F32),
    "nbr": ((32, SLOTS), jnp.int32),
    "codes": ((LIST, 32, SLOTS), F32),
    "hot": ((SLOTS, LIST * SLOTS), BF16),
}


def neighbour(shift, sizes):
    return tuple(
        lax.rem(lax.axis_index(axis) + (d + size), size)
        for (axis, size), d in zip(sizes, shift)
    )


FAR_FIRST = sorted(OTHERS, key=lambda n: -sum(w * abs(d) for w, d in zip((2, 1, 2), SHIFTS[n])))


def kernel(sizes, *refs):
    inputs = refs[:10]
    energy_out, force_out = refs[10:12]
    scratch = dict(zip(SCRATCH, refs[12 : 12 + len(SCRATCH)]))
    refs = refs[12 + len(SCRATCH) :]
    copied, weights = refs[:7], dict(zip(WEIGHTS, refs[:7]))
    packed, table, outbox, inbox, spec_ref, send, recv_near, recv_far, send_back, recv_back, sems = refs[
        7:
    ]
    nbr = scratch["nbr"]

    def remote(src, dst, pair, n):
        return pltpu.make_async_remote_copy(
            src_ref=src,
            dst_ref=dst,
            send_sem=pair[0],
            recv_sem=pair[1],
            device_id=neighbour(SHIFTS[n], sizes),
            device_id_type=MESH,
        )

    own = [
        pltpu.make_async_copy(inputs[1].at[0, 0], spec_ref, sems.at[0]),
        pltpu.make_async_copy(inputs[0].at[:, 0, 0, 0, :], packed.at[0:3], sems.at[1]),
        pltpu.make_async_copy(inputs[2].at[0, 0, :, 0, :], nbr.at[0:LIST, :], sems.at[2]),
    ]
    own += [
        pltpu.make_async_copy(src, dst, sems.at[3 + i])
        for i, (src, dst) in enumerate(zip(inputs[3:], copied))
    ]
    own[0].start()
    own[1].start()
    barrier = pltpu.get_barrier_semaphore()
    for n in FAR_FIRST:
        pl.semaphore_signal(
            barrier, inc=1, device_id=neighbour(SHIFTS[n], sizes), device_id_type=MESH
        )
    for copy in own[2:]:
        copy.start()
    nbr[LIST:, :] = jnp.full((32 - LIST, SLOTS), -1, jnp.int32)
    outbox[:, 3, :] = jnp.zeros((32, SLOTS), F32)
    own[0].wait()
    spec = spec_ref[...]
    packed[3:4, :] = spec.astype(F32)
    own[1].wait()
    pl.semaphore_wait(barrier, 26)

    for n in FAR_FIRST:
        arrived = recv_far if n in FAR else recv_near
        remote(packed, table.at[PLACE[26 - n]], (send, arrived), n).start()
    table[26] = packed[...]
    pos = packed[0:3, :]
    for copy in own[2:]:
        copy.wait()
    prepare_weights(weights, scratch)
    loop(lambda i: prepare_scatter(i, nbr, scratch))
    near, far, everyone = table.at[0 : len(NEAR)], table.at[len(NEAR) : 26], table.at[0:26]
    remote(near, near, (send, recv_near), 0).wait_recv()

    def arrive():
        remote(far, far, (send, recv_far), 0).wait_recv()
        remote(everyone, everyone, (send, recv_far), 0).wait_send()

    energy, center, spread = compute(table, nbr, pos, spec, scratch, arrive)
    for c in range(3):
        outbox[:, c, :] = spread[c * 32 : (c + 1) * 32]
    for n in FAR_FIRST:
        remote(outbox.at[n], inbox.at[PLACE[26 - n]], (send_back, recv_back), n).start()
    energy_out[0, 0] = energy
    force = jnp.concatenate(center, axis=0) - outbox[13, 0:3, :]
    everyone = inbox.at[0:26]
    remote(everyone, everyone, (send_back, recv_back), 0).wait()
    force_out[:, 0, 0, 0, :] = force - total_of([inbox[i, 0:3, :] for i in range(26)])


def solution(mesh):
    sizes = tuple((axis, mesh.shape[axis]) for axis in ("gx", "gy", "gz"))

    def local(positions, species, neighbours, emb_c, emb_n, w_rad, w_two, w_pair, w_lat, w_out):
        vmem = pl.BlockSpec(memory_space=pltpu.VMEM)
        dma = pltpu.SemaphoreType.DMA
        weights = (emb_c, emb_n, w_rad, w_two, w_pair, w_lat.T, w_out.reshape(1, CH))
        return pl.pallas_call(
            functools.partial(kernel, sizes),
            out_shape=(
                pltpu.VMEM(species.shape, F32),
                pltpu.VMEM(positions.shape, F32),
            ),
            in_specs=[pl.BlockSpec(memory_space=pl.ANY)] * 10,
            out_specs=(vmem, vmem),
            scratch_shapes=[pltpu.VMEM(*spec) for spec in SCRATCH.values()]
            + [pltpu.VMEM(w.shape, F32) for w in weights]
            + [
                pltpu.VMEM((4, SLOTS), F32),
                pltpu.VMEM((27, 4, SLOTS), F32),
                pltpu.VMEM((32, 4, SLOTS), F32),
                pltpu.VMEM((26, 4, SLOTS), F32),
                pltpu.VMEM((1, SLOTS), jnp.int32),
            ]
            + [dma] * 5
            + [dma((10,))],
            compiler_params=pltpu.CompilerParams(
                collective_id=0, has_side_effects=True, vmem_limit_bytes=60 << 20
            ),
        )(positions, species, jnp.swapaxes(neighbours, 2, 3), *weights)

    placed = (
        P(None, "gx", "gy", "gz", None),
        P("gx", "gy", "gz", None),
        P("gx", "gy", "gz", None, None),
    ) + (P(),) * 7
    return jax.shard_map(
        local,
        mesh=mesh,
        in_specs=placed,
        out_specs=(P("gx", "gy", "gz", None), P(None, "gx", "gy", "gz", None)),
        check_vma=False,
    )
```
